256 devices in a mesh: depth: 64 (over x, z, core), rows: 4 (over y).
Axes of the slice: x: 4, y: 4, z: 8, core: 2. Of those that a mesh axis runs over, the one named last changes fastest.
Arguments:
- field: float32 [512, 128, 1024], P('depth', 'rows'), may hold values from -4 to 4
- coefficient: float32 [512, 128, 1024], P('depth', 'rows'), may hold values from 0.2 to 1
- rate: float32 [512, 128, 1024], P('depth', 'rows'), may hold values from 1 to 4
Outputs:
- stepped: float32 [512, 128, 1024], P('depth', 'rows')
- image: float32 [4, 128, 1024], P(None, 'rows', 'depth')
The draws below stay inside these ranges and needn't reach their ends.
All inputs are finite; a program needn't handle non-finite values.
Results may differ from the reference program's by a relative error of at most 0.000023.
Values sent between devices are 32-bit elements; how exact they have to be, the bound alone decides.
A program may use at most 64 MiB of HBM per device.

```python
import math
import jax
import jax.numpy as jnp
from jax import lax

NX = 1024
NZ = 512
NY = 128


def levels(own_key, shape, pieces, smallest, high):
    def one(dim, parts):
        heights = jax.random.uniform(jax.random.fold_in(jax.random.fold_in(own_key, 6), dim), (parts,), jnp.float32, smallest / len(pieces), high / len(pieces))
        return jnp.repeat(jnp.exp(heights), shape[dim] // parts).reshape((-1,) + (1,) * (len(shape) - dim - 1))

    gain = one(*pieces[0])
    for cut in pieces[1:]:
        gain = gain * one(*cut)
    return gain


def gaussian(stream_key, dims, scale, bound, cuts=(), kind=jnp.bfloat16):
    values = scale * jax.random.normal(stream_key, dims, jnp.float32)
    if cuts:
        values = values * levels(stream_key, dims, cuts, -0.22, 0.18)
    return jnp.clip(values, -bound, bound).astype(kind)


def setup_inputs(seed: int = 0) -> dict:
    streams_of = jax.random.split(jax.random.key(seed), 4)
    return {
        "field": gaussian(streams_of[0], (NZ, NY, NX), 1.0, 4.0, ((0, 64), (1, 4)), jnp.float32),
        "coefficient": jnp.clip(jnp.exp(math.log(1.0) - 1.609438 * jax.random.uniform(streams_of[1], (NZ, NY, NX), jnp.float32) ** levels(streams_of[1], (NZ, NY, NX), ((0, 64), (1, 4)), -0.2, 0.2)), 0.2, 1.0),
        "rate": jnp.clip(jnp.exp(math.log(4.0) - 1.3862944 * jax.random.uniform(streams_of[2], (NZ, NY, NX), jnp.float32) ** levels(streams_of[2], (NZ, NY, NX), ((0, 64), (1, 4)), -0.2, 0.2)), 1.0, 4.0),
    }


step_size = 0.15

def react(padded, coef_pad, rate_mid):
    upx = jnp.pad(padded, ((0, 0), (0, 0), (1, 1)))
    kpx = jnp.pad(coef_pad, ((0, 0), (0, 0), (1, 1)))
    center = upx[1:-1, 1:-1, 1:-1]
    coef_mid = kpx[1:-1, 1:-1, 1:-1]
    inner = slice(1, -1)
    after = slice(2, None)
    before = slice(None, -2)
    places = [(after, inner, inner), (before, inner, inner), (inner, after, inner), (inner, before, inner), (inner, inner, after), (inner, inner, before)]
    flux = jnp.zeros_like(center)
    for place in places:
        flux = flux + 0.5 * (coef_mid + kpx[place]) * (upx[place] - center)
    return center + step_size * (flux + rate_mid * (jnp.tanh(center) - 0.5 * center))

def shaded(padded, coef_mid, density):
    upx = jnp.pad(padded, ((0, 0), (0, 0), (1, 1)))
    center = upx[1:-1, 1:-1, 1:-1]
    grad_depth = 0.5 * (upx[2:, 1:-1, 1:-1] - upx[:-2, 1:-1, 1:-1])
    grad_row = 0.5 * (upx[1:-1, 2:, 1:-1] - upx[1:-1, :-2, 1:-1])
    grad_col = 0.5 * (upx[1:-1, 1:-1, 2:] - upx[1:-1, 1:-1, :-2])
    norm_sq = grad_depth * grad_depth + grad_row * grad_row + grad_col * grad_col
    facing = jnp.abs(0.48 * grad_depth + 0.6 * grad_row + 0.64 * grad_col) / jnp.sqrt(jnp.maximum(norm_sq, 1.0))
    shading = 0.25 + 0.75 * facing
    opacity = 1.0 - jnp.exp(-density * jax.nn.softplus(2.0 * center))
    weight = opacity * shading
    colour = jnp.stack([weight * jax.nn.sigmoid(2.0 * center), weight * jax.nn.sigmoid(4.0 * coef_mid - 2.0), weight * jax.nn.sigmoid(-2.0 * center), opacity])
    return (opacity, colour)

def reference(field, coefficient, rate):
    widths = ((1, 1), (1, 1), (0, 0))
    coef_pad = jnp.pad(coefficient, widths)
    state = react(jnp.pad(field, widths), coef_pad, rate)
    state = react(jnp.pad(state, widths), coef_pad, rate)
    density = 3.0 / field.shape[0]
    opacity, colour = shaded(jnp.pad(state, widths), coefficient, density)
    through = jnp.cumprod(1.0 - opacity, axis=0)
    transmit = jnp.concatenate([jnp.ones_like(through[:1]), through[:-1]], axis=0)
    image = lax.optimization_barrier(jnp.sum(transmit[None] * colour, axis=1))
    return (state, image)
```

```python
import functools

import jax
import jax.numpy as jnp
from jax import lax
from jax.experimental import pallas as pl
from jax.experimental.pallas import tpu as pltpu
from jax.sharding import PartitionSpec as P

STEP = 0.15
TOP = 8
TILE = 128
BLOCK = 8


def kernel(
    slabs,
    bands,
    f_in,
    k_in,
    r_in,
    stepped,
    image,
    fb,
    kb,
    rb,
    ub,
    sb,
    ax,
    ay,
    sg,
    acc,
    tr,
    xch,
    comb,
    seg,
    load_sem,
    face_send,
    face_recv,
    row_send,
    row_recv,
    pair_send,
    pair_recv,
    part_send,
    part_recv,
):
    d = lax.axis_index("depth")
    y = lax.axis_index("rows")
    planes, lines, columns = f_in.shape
    chips = slabs // 2
    width = columns // slabs
    tiles = columns // TILE
    per_tile = chips // tiles
    core = lax.rem(d, 2)
    chip = d // 2
    last = planes + 1
    low, high = TOP, TOP + lines
    density = 3.0 / (planes * slabs)
    body_rows = slice(low, high)

    loads = [
        pltpu.make_async_copy(src, dst, load_sem.at[i])
        for i, (src, dst) in enumerate(
            [
                (k_in, kb.at[1:last, body_rows, :]),
                (f_in, fb.at[1:last, body_rows, :]),
                (r_in, rb),
            ]
        )
    ]
    for copy in loads:
        copy.start()

    barrier = pltpu.get_barrier_semaphore()
    for other in (lax.rem(d + 1, slabs), lax.rem(d + slabs - 1, slabs)):
        pl.semaphore_signal(barrier, inc=1, device_id={"depth": other})
    for other in (lax.rem(y + 1, bands), lax.rem(y + bands - 1, bands)):
        pl.semaphore_signal(barrier, inc=1, device_id={"rows": other})

    def greet(i, carry):
        other = lax.rem(chip + i, chips)
        pl.semaphore_signal(barrier, inc=1, device_id={"depth": other * 2 + core})
        return carry

    lax.fori_loop(1, chips, greet, 0)

    def clear_planes(plane):
        for buf in (fb, kb, ub, sb):
            buf[plane, body_rows, :] = jnp.zeros((lines, columns), jnp.float32)

    def clear_rows(row):
        for buf in (fb, kb, ub, sb):
            buf[1:last, row : row + 1, :] = jnp.zeros((planes, 1, columns), jnp.float32)

    pl.when(d == 0)(lambda: clear_planes(0))
    pl.when(d == slabs - 1)(lambda: clear_planes(last))
    pl.when(y == 0)(lambda: clear_rows(low - 1))
    pl.when(y == bands - 1)(lambda: clear_rows(high))
    pl.semaphore_wait(barrier, chips + 3)

    def to_front(src, dst, n):
        return pltpu.make_async_remote_copy(
            src, dst.at[last, body_rows, :], face_send.at[n, 0], face_recv.at[n, 0], device_id={"depth": d - 1}
        )

    def to_back(src, dst, n):
        return pltpu.make_async_remote_copy(
            src, dst.at[0, body_rows, :], face_send.at[n, 1], face_recv.at[n, 1], device_id={"depth": d + 1}
        )

    def to_above(src, dst, a, b, n):
        return pltpu.make_async_remote_copy(
            src, dst.at[a:b, high : high + 1, :], row_send.at[n, 0], row_recv.at[n, 0], device_id={"rows": y - 1}
        )

    def to_below(src, dst, a, b, n):
        return pltpu.make_async_remote_copy(
            src, dst.at[a:b, low - 1 : low, :], row_send.at[n, 1], row_recv.at[n, 1], device_id={"rows": y + 1}
        )

    def face_copies(buf, n, src=None):
        first = buf.at[1, body_rows, :] if src is None else src.at[0]
        final = buf.at[planes, body_rows, :] if src is None else src.at[planes - 1]
        return to_front(first, buf, n), to_back(final, buf, n)

    def row_copies(buf, a, b, n, src=None):
        first = buf.at[a:b, low : low + 1, :] if src is None else src.at[:, 0:1, :]
        final = buf.at[a:b, high - 1 : high, :] if src is None else src.at[:, lines - 1 : lines, :]
        return to_above(first, buf, a, b, n), to_below(final, buf, a, b, n)

    def start_faces(copies):
        pl.when(d > 0)(lambda: copies[0].start())
        pl.when(d < slabs - 1)(lambda: copies[1].start())

    def start_rows(copies):
        pl.when(y > 0)(lambda: copies[0].start())
        pl.when(y < bands - 1)(lambda: copies[1].start())

    def arrive_faces(copies):
        pl.when(d < slabs - 1)(lambda: copies[0].wait_recv())
        pl.when(d > 0)(lambda: copies[1].wait_recv())

    def arrive_rows(copies):
        pl.when(y < bands - 1)(lambda: copies[0].wait_recv())
        pl.when(y > 0)(lambda: copies[1].wait_recv())

    def sent_faces(copies):
        pl.when(d > 0)(lambda: copies[0].wait_send())
        pl.when(d < slabs - 1)(lambda: copies[1].wait_send())

    def sent_rows(copies):
        pl.when(y > 0)(lambda: copies[0].wait_send())
        pl.when(y < bands - 1)(lambda: copies[1].wait_send())

    faces = [face_copies(fb, 0, f_in), face_copies(kb, 1, k_in), face_copies(ub, 2), face_copies(sb, 3)]
    rows = [
        row_copies(fb, 1, last, 0, f_in),
        row_copies(kb, 1, last, 1, k_in),
        row_copies(ub, 2, planes, 2),
        row_copies(ub, 1, 2, 3),
        row_copies(ub, planes, last, 4),
        row_copies(sb, 2, planes, 5),
        row_copies(sb, 1, 2, 6),
        row_copies(sb, planes, last, 7),
    ]
    start_rows(rows[0])
    start_rows(rows[1])
    start_faces(faces[0])
    start_faces(faces[1])

    lane = lax.broadcasted_iota(jnp.int32, (BLOCK, columns), 1)
    at_start = lane == 0
    at_end = lane == columns - 1
    blocks = [low + BLOCK * i for i in range(lines // BLOCK)]

    loads[0].wait()

    def prepare(p, carry):
        for r in blocks:
            k = kb[p + 1, r : r + BLOCK, :]
            ax[p, r - low : r - low + BLOCK, :] = k + jnp.where(at_end, 0.0, pltpu.roll(k, columns - 1, 1))
            sg[p, r - low : r - low + BLOCK, :] = 0.5 + 0.5 * jnp.tanh(2.0 * k - 1.0)
        return carry

    lax.fori_loop(0, planes, prepare, 0)
    loads[1].wait()
    loads[2].wait()
    arrive_rows(rows[0])
    arrive_rows(rows[1])

    def prepare_rows(p, carry):
        for r in blocks:
            ay[p, r : r + BLOCK, :] = kb[p + 1, r : r + BLOCK, :] + kb[p + 1, r + 1 : r + 1 + BLOCK, :]
        ay[p, low - 1 : low, :] = kb[p + 1, low - 1 : low, :] + kb[p + 1, low : low + 1, :]
        return carry

    lax.fori_loop(0, planes, prepare_rows, 0)

    def react(src, dst, p):
        for r in blocks:
            here = slice(r, r + BLOCK)
            above = slice(r - 1, r - 1 + BLOCK)
            below = slice(r + 1, r + 1 + BLOCK)
            local = slice(r - low, r - low + BLOCK)
            u = src[p + 1, here, :]
            k = kb[p + 1, here, :]
            flux = (k + kb[p, here, :]) * (src[p, here, :] - u)
            flux = flux + (k + kb[p + 2, here, :]) * (src[p + 2, here, :] - u)
            flux = flux + ay[p, here, :] * (src[p + 1, below, :] - u)
            flux = flux + ay[p, above, :] * (src[p + 1, above, :] - u)
            right = jnp.where(at_end, 0.0, pltpu.roll(u, columns - 1, 1))
            out = ax[p, local, :] * (right - u)
            flux = flux + (out - jnp.where(at_start, k * u, pltpu.roll(out, 1, 1)))
            rate = STEP * rb[p, local, :]
            dst[p + 1, here, :] = u + (0.5 * STEP) * flux + rate * (jnp.tanh(u) - 0.5 * u)

    def over(start, count, stride, body):
        def lap(i, carry):
            body(start + stride * i)
            return carry

        lax.fori_loop(0, count, lap, 0)

    inner = (1, planes - 2, 1)
    outer = (0, 2, planes - 1)

    over(*inner, lambda p: react(fb, ub, p))
    start_rows(rows[2])
    arrive_faces(faces[0])
    arrive_faces(faces[1])
    over(*outer, lambda p: react(fb, ub, p))
    start_faces(faces[2])
    start_rows(rows[3])
    start_rows(rows[4])

    arrive_rows(rows[2])
    over(*inner, lambda p: react(ub, sb, p))
    start_rows(rows[5])
    arrive_faces(faces[2])
    arrive_rows(rows[3])
    arrive_rows(rows[4])
    over(*outer, lambda p: react(ub, sb, p))
    start_faces(faces[3])
    start_rows(rows[6])
    start_rows(rows[7])
    store = pltpu.make_async_copy(sb.at[1:last, body_rows, :], stepped, load_sem.at[3])
    store.start()

    def shade(p, r):
        here = slice(r, r + BLOCK)
        u = sb[p + 1, here, :]
        g_depth = sb[p + 2, here, :] - sb[p, here, :]
        g_row = sb[p + 1, r + 1 : r + 1 + BLOCK, :] - sb[p + 1, r - 1 : r - 1 + BLOCK, :]
        right = jnp.where(at_end, 0.0, pltpu.roll(u, columns - 1, 1))
        left = jnp.where(at_start, 0.0, pltpu.roll(u, 1, 1))
        g_col = right - left
        norm = g_depth * g_depth + g_row * g_row + g_col * g_col
        facing = jnp.abs(0.36 * g_depth + 0.45 * g_row + 0.48 * g_col) * lax.rsqrt(jnp.maximum(norm, 4.0))
        rise = jnp.exp(2.0 * u)
        whole = 1.0 + rise
        passed = jnp.exp(-density * jnp.log(whole))
        weight = (1.0 - passed) * (0.25 + facing)
        red = weight * (rise / whole)
        green = weight * sg[p, r - low : r - low + BLOCK, :]
        return red, green, weight - red, passed

    def shade_inner(p):
        for r in blocks:
            local = slice(r - low, r - low + BLOCK)
            through = acc[3, local, :]
            red, green, blue, passed = shade(p, r)
            acc[0, local, :] += through * red
            acc[1, local, :] += through * green
            acc[2, local, :] += through * blue
            acc[3, local, :] = through * passed

    acc[0:3] = jnp.zeros((3, lines, columns), jnp.float32)
    acc[3] = jnp.ones((lines, columns), jnp.float32)
    arrive_rows(rows[5])
    over(*inner, shade_inner)
    arrive_faces(faces[3])
    arrive_rows(rows[6])
    arrive_rows(rows[7])

    for r in blocks:
        local = slice(r - low, r - low + BLOCK)
        front = shade(0, r)
        back = shade(planes - 1, r)
        through = front[3] * acc[3, local, :]
        for c in range(3):
            acc[c, local, :] = front[c] + front[3] * acc[c, local, :] + through * back[c]
        acc[3, local, :] = through * back[3]

    def pair_copy(t):
        part = pl.ds(t * per_tile, per_tile)
        return pltpu.make_async_remote_copy(
            tr.at[part, 1 - core],
            xch.at[part],
            pair_send.at[t],
            pair_recv.at[t],
            device_id={"depth": chip * 2 + 1 - core},
        )

    first_tile = chip // per_tile

    def turn(i, carry):
        t = lax.rem(first_tile + i, tiles)
        cols = pl.ds(pl.multiple_of(t * TILE, TILE), TILE)
        stack = jnp.concatenate([acc[c, :, cols] for c in range(4)], axis=0)
        tr[pl.ds(t * per_tile, per_tile)] = stack.T.reshape(per_tile, 2, width, 4 * lines)
        pair_copy(t).start()
        return carry

    lax.fori_loop(0, tiles, turn, 0)

    small = lax.broadcasted_iota(jnp.int32, (width, 4 * lines), 1)
    colour_lane = small < 3 * lines

    def spread(x):
        half = jnp.where(small >= 3 * lines, x, pltpu.roll(x, 3 * lines, 1))
        return jnp.where(small >= 2 * lines, half, pltpu.roll(half, 2 * lines, 1))

    def part_copy(to, slot):
        return pltpu.make_async_remote_copy(
            comb.at[to], seg.at[slot], part_send.at[to], part_recv.at[slot], device_id={"depth": to * 2 + core}
        )

    def join(i, carry):
        t = lax.rem(first_tile + i, tiles)
        pair_copy(t).wait_recv()
        for q in range(per_tile):
            m = t * per_tile + q
            mine = tr[m, core]
            other = xch[m]
            front = jnp.where(core == 0, mine, other)
            back = jnp.where(core == 0, other, mine)
            comb[m] = spread(front) * back + jnp.where(colour_lane, front, 0.0)
        for q in range(per_tile):
            m = t * per_tile + q
            pl.when(m != chip)(lambda: part_copy(m, chip).start())
        return carry

    lax.fori_loop(0, tiles, join, 0)
    seg[chip] = comb[chip]

    def gather(m, carry):
        total, through = carry
        pl.when(m != chip)(lambda: part_copy(m, m).wait_recv())
        piece = seg[m]
        return total + through * piece, through * spread(piece)

    shape = (width, 4 * lines)
    total, through = lax.fori_loop(0, chips, gather, (jnp.zeros(shape, jnp.float32), jnp.ones(shape, jnp.float32)))
    result = jnp.where(colour_lane, total, 1.0 - through)
    for c in range(4):
        image[c] = result[:, c * lines : (c + 1) * lines]

    def finish(m, carry):
        pl.when(m != chip)(lambda: part_copy(m, chip).wait_send())
        return carry

    lax.fori_loop(0, chips, finish, 0)

    def finish_pairs(t, carry):
        pair_copy(t).wait_send()
        return carry

    lax.fori_loop(0, tiles, finish_pairs, 0)
    for copies in faces:
        sent_faces(copies)
    for copies in rows:
        sent_rows(copies)
    store.wait()


def on_device(slabs, bands, field, coefficient, rate):
    planes, lines, columns = field.shape
    chips = slabs // 2
    width = columns // slabs
    padded = pltpu.VMEM((planes + 2, lines + 2 * TOP, columns), jnp.float32)
    plain = pltpu.VMEM((planes, lines, columns), jnp.float32)
    parts = pltpu.VMEM((chips, width, 4 * lines), jnp.float32)
    dma = pltpu.SemaphoreType.DMA
    stepped, image = pl.pallas_call(
        functools.partial(kernel, slabs, bands),
        out_shape=(
            jax.ShapeDtypeStruct(field.shape, jnp.float32),
            jax.ShapeDtypeStruct((4, width, lines), jnp.float32),
        ),
        in_specs=[pl.BlockSpec(memory_space=pltpu.HBM)] * 3,
        out_specs=(pl.BlockSpec(memory_space=pl.ANY), pl.BlockSpec(memory_space=pltpu.VMEM)),
        scratch_shapes=[
            padded,
            padded,
            plain,
            padded,
            padded,
            plain,
            pltpu.VMEM((planes, lines + 2 * TOP, columns), jnp.float32),
            plain,
            pltpu.VMEM((4, lines, columns), jnp.float32),
            pltpu.VMEM((chips, 2, width, 4 * lines), jnp.float32),
            parts,
            parts,
            parts,
            dma((4,)),
            dma((4, 2)),
            dma((4, 2)),
            dma((8, 2)),
            dma((8, 2)),
            dma((columns // TILE,)),
            dma((columns // TILE,)),
            dma((chips,)),
            dma((chips,)),
        ],
        compiler_params=pltpu.CompilerParams(collective_id=0, has_side_effects=True, vmem_limit_bytes=62 << 20),
    )(field, coefficient, rate)
    return stepped, jnp.swapaxes(image, 1, 2)


def solution(mesh):
    return jax.shard_map(
        functools.partial(on_device, mesh.shape["depth"], mesh.shape["rows"]),
        mesh=mesh,
        in_specs=(P("depth", "rows", None),) * 3,
        out_specs=(P("depth", "rows", None), P(None, "rows", "depth")),
        check_vma=False,
    )
```

```python
import functools

import jax
import jax.numpy as jnp
from jax import lax
from jax.experimental import pallas as pl
from jax.experimental.pallas import tpu as pltpu
from jax.sharding import PartitionSpec as P

STEP = 0.15
TOP = 8
TILE = 128
BLOCK = 8
CHUNKS = 1
RING = 8


def kernel(
    slabs,
    bands,
    f_in,
    k_in,
    r_in,
    stepped,
    image,
    fb,
    kb,
    rb,
    ub,
    sb,
    ax,
    ay,
    sg,
    acc,
    gc,
    cf,
    cb,
    pieces,
    front_pass,
    comb,
    seg,
    load_sem,
    face_send,
    face_recv,
    row_send,
    row_recv,
    pair_send,
    pair_recv,
    part_send,
    part_recv,
    pass_sem,
    known,
):
    d = lax.axis_index("depth")
    y = lax.axis_index("rows")
    planes, lines, columns = f_in.shape
    chips = slabs // 2
    width = columns // slabs
    tiles = columns // TILE
    per_tile = chips // tiles
    core = lax.rem(d, 2)
    chip = d // 2
    last = planes + 1
    low, high = TOP, TOP + lines
    density = 3.0 / (planes * slabs)
    body_rows = slice(low, high)
    spans = [slice(i * columns // CHUNKS, (i + 1) * columns // CHUNKS) for i in range(CHUNKS)]

    loads = [
        pltpu.make_async_copy(src, dst, load_sem.at[i])
        for i, (src, dst) in enumerate(
            [
                (k_in, kb.at[1:last, body_rows, :]),
                (f_in, fb.at[1:last, body_rows, :]),
                (r_in, rb),
            ]
        )
    ]
    for copy in loads:
        copy.start()

    barrier = pltpu.get_barrier_semaphore()
    x, z = chip // RING, lax.rem(chip, RING)
    lanes_x = chips // RING

    def along_z(step):
        return (x * RING + lax.rem(z + step, RING)) * 2 + core

    def along_x(step):
        return (lax.rem(x + step, lanes_x) * RING + z) * 2 + core

    z_next, z_prev = along_z(1), along_z(RING - 1)
    x_next, x_prev = along_x(1), along_x(lanes_x - 1)
    for other in (lax.rem(d + 1, slabs), lax.rem(d + slabs - 1, slabs), z_next, z_prev, x_next, x_prev):
        pl.semaphore_signal(barrier, inc=1, device_id={"depth": other})
    for other in (lax.rem(y + 1, bands), lax.rem(y + bands - 1, bands)):
        pl.semaphore_signal(barrier, inc=1, device_id={"rows": other})

    z_rounds = RING // 2 - 1
    rounds = z_rounds + lanes_x // 2

    def tell(n):
        after, before = (z_next, z_prev) if n < z_rounds else (x_next, x_prev)
        pl.semaphore_signal(known.at[n, 0], inc=1, device_id={"depth": after})
        pl.semaphore_signal(known.at[n, 1], inc=1, device_id={"depth": before})

    def hear(n):
        pl.semaphore_wait(known.at[n, 0], 1)
        pl.semaphore_wait(known.at[n, 1], 1)

    def clear_planes(plane):
        for buf in (fb, kb, ub, sb):
            buf[plane, body_rows, :] = jnp.zeros((lines, columns), jnp.float32)

    def clear_rows(row):
        for buf in (fb, kb, ub, sb):
            buf[1:last, row : row + 1, :] = jnp.zeros((planes, 1, columns), jnp.float32)

    pl.when(d == 0)(lambda: clear_planes(0))
    pl.when(d == slabs - 1)(lambda: clear_planes(last))
    pl.when(y == 0)(lambda: clear_rows(low - 1))
    pl.when(y == bands - 1)(lambda: clear_rows(high))
    pl.semaphore_wait(barrier, 8)

    def to_front(src, dst, n, c):
        return pltpu.make_async_remote_copy(
            src, dst.at[last, body_rows, spans[c]], face_send.at[n, 0, c], face_recv.at[n, 0, c], device_id={"depth": d - 1}
        )

    def to_back(src, dst, n, c):
        return pltpu.make_async_remote_copy(
            src, dst.at[0, body_rows, spans[c]], face_send.at[n, 1, c], face_recv.at[n, 1, c], device_id={"depth": d + 1}
        )

    def to_above(src, dst, a, b, n):
        return pltpu.make_async_remote_copy(
            src, dst.at[a:b, high : high + 1, :], row_send.at[n, 0], row_recv.at[n, 0], device_id={"rows": y - 1}
        )

    def to_below(src, dst, a, b, n):
        return pltpu.make_async_remote_copy(
            src, dst.at[a:b, low - 1 : low, :], row_send.at[n, 1], row_recv.at[n, 1], device_id={"rows": y + 1}
        )

    def face_copies(buf, n, c, src=None):
        first = buf.at[1, body_rows, spans[c]] if src is None else src.at[0, :, spans[c]]
        final = buf.at[planes, body_rows, spans[c]] if src is None else src.at[planes - 1, :, spans[c]]
        return to_front(first, buf, n, c), to_back(final, buf, n, c)

    def row_copies(buf, a, b, n, src=None):
        first = buf.at[a:b, low : low + 1, :] if src is None else src.at[:, 0:1, :]
        final = buf.at[a:b, high - 1 : high, :] if src is None else src.at[:, lines - 1 : lines, :]
        return to_above(first, buf, a, b, n), to_below(final, buf, a, b, n)

    def start_faces(copies):
        pl.when(d > 0)(lambda: copies[0].start())
        pl.when(d < slabs - 1)(lambda: copies[1].start())

    def start_rows(copies):
        pl.when(y > 0)(lambda: copies[0].start())
        pl.when(y < bands - 1)(lambda: copies[1].start())

    def arrive_faces(copies):
        pl.when(d < slabs - 1)(lambda: copies[0].wait_recv())
        pl.when(d > 0)(lambda: copies[1].wait_recv())

    def arrive_rows(copies):
        pl.when(y < bands - 1)(lambda: copies[0].wait_recv())
        pl.when(y > 0)(lambda: copies[1].wait_recv())

    def sent_faces(copies):
        pl.when(d > 0)(lambda: copies[0].wait_send())
        pl.when(d < slabs - 1)(lambda: copies[1].wait_send())

    def sent_rows(copies):
        pl.when(y > 0)(lambda: copies[0].wait_send())
        pl.when(y < bands - 1)(lambda: copies[1].wait_send())

    faces = [
        [face_copies(buf, n, c, src) for c in range(CHUNKS)]
        for n, (buf, src) in enumerate([(fb, f_in), (kb, k_in), (ub, None), (sb, None)])
    ]
    rows = [
        row_copies(fb, 1, last, 0, f_in),
        row_copies(kb, 1, last, 1, k_in),
        row_copies(ub, 2, planes, 2),
        row_copies(ub, 1, 2, 3),
        row_copies(ub, planes, last, 4),
        row_copies(sb, 2, planes, 5),
        row_copies(sb, 1, 2, 6),
        row_copies(sb, planes, last, 7),
    ]
    for c in range(CHUNKS):
        start_faces(faces[0][c])
        start_faces(faces[1][c])
    start_rows(rows[0])
    start_rows(rows[1])
    tell(0)

    def window(c):
        if c is None:
            return 0, columns, 0, columns
        near, far = spans[c].start, spans[c].stop
        return max(near - TILE, 0), min(far + TILE, columns), near, far

    def edges(a, b):
        lane = lax.broadcasted_iota(jnp.int32, (BLOCK, b - a), 1) + a
        return lane == 0, lane == columns - 1

    _, at_end = edges(0, columns)
    blocks = [low + BLOCK * i for i in range(lines // BLOCK)]

    loads[0].wait()

    def prepare(p, carry):
        for r in blocks:
            k = kb[p + 1, r : r + BLOCK, :]
            ax[p, r - low : r - low + BLOCK, :] = k + jnp.where(at_end, 0.0, pltpu.roll(k, columns - 1, 1))
            sg[p, r - low : r - low + BLOCK, :] = 0.5 + 0.5 * jnp.tanh(2.0 * k - 1.0)
        return carry

    lax.fori_loop(0, planes, prepare, 0)
    hear(0)
    tell(1)
    loads[1].wait()
    loads[2].wait()
    arrive_rows(rows[0])
    arrive_rows(rows[1])

    def prepare_rows(p, carry):
        for r in blocks:
            ay[p, r : r + BLOCK, :] = kb[p + 1, r : r + BLOCK, :] + kb[p + 1, r + 1 : r + 1 + BLOCK, :]
        ay[p, low - 1 : low, :] = kb[p + 1, low - 1 : low, :] + kb[p + 1, low : low + 1, :]
        return carry

    lax.fori_loop(0, planes, prepare_rows, 0)

    def react(src, dst, p, c=None):
        a, b, near, far = window(c)
        wide, keep = slice(a, b), slice(near - a, far - a)
        at_start, at_end = edges(a, b)
        for r in blocks:
            here = slice(r, r + BLOCK), wide
            local = slice(r - low, r - low + BLOCK), wide
            u = src[p + 1, *here]
            k = kb[p + 1, *here]
            right = jnp.where(at_end, 0.0, pltpu.roll(u, b - a - 1, 1))
            out = ax[p, *local] * (right - u)
            flux = (out - jnp.where(at_start, k * u, pltpu.roll(out, 1, 1)))[:, keep]
            u, k = u[:, keep], k[:, keep]
            here = slice(r, r + BLOCK), slice(near, far)
            above = slice(r - 1, r - 1 + BLOCK), slice(near, far)
            below = slice(r + 1, r + 1 + BLOCK), slice(near, far)
            local = slice(r - low, r - low + BLOCK), slice(near, far)
            flux = flux + (k + kb[p, *here]) * (src[p, *here] - u)
            flux = flux + (k + kb[p + 2, *here]) * (src[p + 2, *here] - u)
            flux = flux + ay[p, *here] * (src[p + 1, *below] - u)
            flux = flux + ay[p, *above] * (src[p + 1, *above] - u)
            rate = STEP * rb[p, *local]
            dst[p + 1, *here] = u + (0.5 * STEP) * flux + rate * (jnp.tanh(u) - 0.5 * u)

    def over(start, count, stride, body):
        def lap(i, carry):
            body(start + stride * i)
            return carry

        lax.fori_loop(0, count, lap, 0)

    inner = (1, planes - 2, 1)
    outer = (0, 2, planes - 1)

    over(*inner, lambda p: react(fb, ub, p))
    start_rows(rows[2])
    hear(1)
    tell(2)
    for c in range(CHUNKS):
        arrive_faces(faces[0][c])
        arrive_faces(faces[1][c])
        over(*outer, lambda p: react(fb, ub, p, c))
        start_faces(faces[2][c])
    start_rows(rows[3])
    start_rows(rows[4])
    hear(2)
    tell(3)

    arrive_rows(rows[2])
    over(*inner, lambda p: react(ub, sb, p))
    start_rows(rows[5])
    hear(3)
    tell(4)
    for c in range(CHUNKS):
        arrive_faces(faces[2][c])
        if c == 0:
            arrive_rows(rows[3])
            arrive_rows(rows[4])
        over(*outer, lambda p: react(ub, sb, p, c))
        start_faces(faces[3][c])
    start_rows(rows[6])
    start_rows(rows[7])
    store = pltpu.make_async_copy(sb.at[1:last, body_rows, :], stepped, load_sem.at[3])
    store.start()

    def lit(g_depth, g_row, g_col):
        norm = g_depth * g_depth + g_row * g_row + g_col * g_col
        facing = jnp.abs(0.36 * g_depth + 0.45 * g_row + 0.48 * g_col)
        return 0.25 + facing * lax.rsqrt(jnp.maximum(norm, 4.0))

    def across(p, r):
        u = sb[p + 1, r : r + BLOCK, :]
        at_start, at_end = edges(0, columns)
        right = jnp.where(at_end, 0.0, pltpu.roll(u, columns - 1, 1))
        return right - jnp.where(at_start, 0.0, pltpu.roll(u, 1, 1))

    def matter(p, r):
        rise = jnp.exp(2.0 * sb[p + 1, r : r + BLOCK, :])
        whole = 1.0 + rise
        passed = jnp.exp(-density * jnp.log(whole))
        opacity = 1.0 - passed
        return opacity, opacity * (rise / whole), opacity * sg[p, r - low : r - low + BLOCK, :], passed

    def shade(p, r):
        here = slice(r, r + BLOCK)
        g_depth = sb[p + 2, here, :] - sb[p, here, :]
        g_row = sb[p + 1, r + 1 : r + 1 + BLOCK, :] - sb[p + 1, r - 1 : r - 1 + BLOCK, :]
        light = lit(g_depth, g_row, across(p, r))
        opacity, red, green, passed = matter(p, r)
        red = light * red
        return red, light * green, light * opacity - red, passed

    def shade_inner(p):
        for r in blocks:
            local = slice(r - low, r - low + BLOCK)
            through = acc[3, local, :]
            red, green, blue, passed = shade(p, r)
            acc[0, local, :] += through * red
            acc[1, local, :] += through * green
            acc[2, local, :] += through * blue
            acc[3, local, :] = through * passed

    acc[0:3] = jnp.zeros((3, lines, columns), jnp.float32)
    acc[3] = jnp.ones((lines, columns), jnp.float32)
    arrive_rows(rows[5])
    over(*inner, shade_inner)
    for r in blocks:
        local = slice(r - low, r - low + BLOCK)
        gc[0, local, :] = across(0, r)
        gc[1, local, :] = across(planes - 1, r)
        opacity, red, green, passed = matter(0, r)
        cf[0, local, :] = red
        cf[1, local, :] = green
        cf[2, local, :] = opacity - red
        for i in range(3):
            acc[i, local, :] = passed * acc[i, local, :]
        through = passed * acc[3, local, :]
        opacity, red, green, passed = matter(planes - 1, r)
        red = through * red
        cb[0, local, :] = red
        cb[1, local, :] = through * green
        cb[2, local, :] = through * opacity - red
        acc[3, local, :] = through * passed

    partner = {"depth": chip * 2 + 1 - core}

    def pair_copy(t):
        part = pl.ds(t * per_tile, per_tile)
        return pltpu.make_async_remote_copy(
            pieces.at[part, 2], pieces.at[part, core], pair_send.at[t], pair_recv.at[t], device_id=partner
        )

    order = []
    for i in (lanes_x // 2, 1, lanes_x - 1, 0):
        for h in (1, 0):
            side = lax.rem(z // per_tile + h, 2)
            order.append(lax.rem(x + i, lanes_x) * 2 + side)

    def span(t):
        return pl.ds(pl.multiple_of(t * TILE, TILE), TILE)

    pass_copy = pltpu.make_async_remote_copy(
        front_pass.at[1], front_pass.at[1], pass_sem.at[0], pass_sem.at[1], device_id=partner
    )

    @pl.when(core == 0)
    def _():
        for t in range(tiles):
            stack = jnp.concatenate([acc[3, :, t * TILE : (t + 1) * TILE]] * 4, axis=0)
            turned = stack.T.reshape(per_tile, 2, width, 4 * lines)
            part = slice(t * per_tile, (t + 1) * per_tile)
            front_pass[0, part] = turned[:, 0]
            front_pass[1, part] = turned[:, 1]
        pass_copy.start()

    arrive_faces(faces[3][0])
    arrive_rows(rows[6])
    arrive_rows(rows[7])

    def light_of(p, q, cols):
        g_depth = sb[p + 2, body_rows, cols] - sb[p, body_rows, cols]
        g_row = sb[p + 1, low + 1 : high + 1, cols] - sb[p + 1, low - 1 : high - 1, cols]
        return lit(g_depth, g_row, gc[q, :, cols])

    for t in order:
        cols = span(t)
        first = light_of(0, 0, cols)
        final = light_of(planes - 1, 1, cols)
        stack = [acc[c, :, cols] + first * cf[c, :, cols] + final * cb[c, :, cols] for c in range(3)]
        stack = jnp.concatenate(stack + [acc[3, :, cols]], axis=0)
        turned = stack.T.reshape(per_tile, 2, width, 4 * lines)
        part = pl.ds(t * per_tile, per_tile)
        pieces[part, 2 * core] = turned[:, 0]
        pieces[part, 2 - core] = turned[:, 1]
        pair_copy(t).start()

    small = lax.broadcasted_iota(jnp.int32, (width, 4 * lines), 1)
    colour_lane = small < 3 * lines

    def spread(x):
        half = jnp.where(small >= 3 * lines, x, pltpu.roll(x, 3 * lines, 1))
        return jnp.where(small >= 2 * lines, half, pltpu.roll(half, 2 * lines, 1))

    def part_copy(to, slot):
        return pltpu.make_async_remote_copy(
            comb.at[to], seg.at[slot], part_send.at[0], part_recv.at[0], device_id={"depth": to * 2 + core}
        )

    def all_parts():
        others = pl.ds(0, chips - 1)
        return pltpu.make_async_remote_copy(
            comb.at[others], seg.at[others], part_send.at[0], part_recv.at[0], device_id={"depth": d}
        )

    hear(rounds - 1)
    pl.when(core == 1)(lambda: pass_copy.wait_recv())
    for t in order:
        pair_copy(t).wait_recv()
        for q in range(per_tile):
            m = t * per_tile + q
            front = pieces[m, 0]
            comb[m] = front_pass[core, m] * pieces[m, 1] + jnp.where(colour_lane, front, 0.0)
        for q in range(per_tile):
            m = t * per_tile + q
            pl.when(m != chip)(lambda: part_copy(m, chip).start())
    seg[chip] = comb[chip]

    shape = (width, 4 * lines)
    all_parts().wait_recv()
    total, through = jnp.zeros(shape, jnp.float32), jnp.ones(shape, jnp.float32)
    for m in range(chips):
        piece = seg[m]
        total = total + through * piece
        through = through * spread(piece)
    result = jnp.where(colour_lane, total, 1.0 - through)
    for c in range(4):
        image[c] = result[:, c * lines : (c + 1) * lines]

    all_parts().wait_send()

    def finish_pairs(t, carry):
        pair_copy(t).wait_send()
        return carry

    lax.fori_loop(0, tiles, finish_pairs, 0)
    pl.when(core == 0)(lambda: pass_copy.wait_send())
    for copies in sum(faces, []):
        sent_faces(copies)
    for copies in rows:
        sent_rows(copies)
    store.wait()


def on_device(slabs, bands, field, coefficient, rate):
    planes, lines, columns = field.shape
    chips = slabs // 2
    width = columns // slabs
    padded = pltpu.VMEM((planes + 2, lines + 2 * TOP, columns), jnp.float32)
    plain = pltpu.VMEM((planes, lines, columns), jnp.float32)
    parts = pltpu.VMEM((chips, width, 4 * lines), jnp.float32)
    dma = pltpu.SemaphoreType.DMA
    stepped, image = pl.pallas_call(
        functools.partial(kernel, slabs, bands),
        out_shape=(
            jax.ShapeDtypeStruct(field.shape, jnp.float32),
            jax.ShapeDtypeStruct((4, width, lines), jnp.float32),
        ),
        in_specs=[pl.BlockSpec(memory_space=pltpu.HBM)] * 3,
        out_specs=(pl.BlockSpec(memory_space=pl.ANY), pl.BlockSpec(memory_space=pltpu.VMEM)),
        scratch_shapes=[
            padded,
            padded,
            plain,
            padded,
            padded,
            plain,
            pltpu.VMEM((planes, lines + 2 * TOP, columns), jnp.float32),
            plain,
            pltpu.VMEM((4, lines, columns), jnp.float32),
            pltpu.VMEM((2, lines, columns), jnp.float32),
            pltpu.VMEM((3, lines, columns), jnp.float32),
            pltpu.VMEM((3, lines, columns), jnp.float32),
            pltpu.VMEM((chips, 3, width, 4 * lines), jnp.float32),
            pltpu.VMEM((2, chips, width, 4 * lines), jnp.float32),
            parts,
            parts,
            dma((4,)),
            dma((4, 2, CHUNKS)),
            dma((4, 2, CHUNKS)),
            dma((8, 2)),
            dma((8, 2)),
            dma((columns // TILE,)),
            dma((columns // TILE,)),
            dma((1,)),
            dma((1,)),
            dma((2,)),
            pltpu.SemaphoreType.REGULAR((chips // RING // 2 + RING // 2 - 1, 2)),
        ],
        compiler_params=pltpu.CompilerParams(collective_id=0, has_side_effects=True, vmem_limit_bytes=40 << 20),
    )(*(pltpu.with_memory_space_constraint(v, pltpu.HBM) for v in (field, coefficient, rate)))
    return stepped, jnp.swapaxes(image, 1, 2)


def solution(mesh):
    return jax.shard_map(
        functools.partial(on_device, mesh.shape["depth"], mesh.shape["rows"]),
        mesh=mesh,
        in_specs=(P("depth", "rows", None),) * 3,
        out_specs=(P("depth", "rows", None), P(None, "rows", "depth")),
        check_vma=False,
    )
```

```python
import functools

import jax
import jax.numpy as jnp
from jax import lax
from jax.experimental import pallas as pl
from jax.experimental.pallas import tpu as pltpu
from jax.sharding import PartitionSpec as P

STEP = 0.15
TOP = 8
TILE = 128
BLOCK = 8
RING = 8


def kernel(
    slabs,
    bands,
    f_in,
    k_in,
    r_in,
    stepped,
    image,
    fb,
    kb,
    rb,
    ub,
    sb,
    ax,
    ay,
    sg,
    acc,
    gc,
    ends,
    pieces,
    front_pass,
    comb,
    seg,
    load_sem,
    face_send,
    face_recv,
    row_send,
    row_recv,
    pair_send,
    pair_recv,
    part_send,
    part_recv,
    pass_sem,
    known,
):
    d = lax.axis_index("depth")
    y = lax.axis_index("rows")
    planes, lines, columns = f_in.shape
    chips = slabs // 2
    width = columns // slabs
    tiles = columns // TILE
    per_tile = chips // tiles
    core = lax.rem(d, 2)
    chip = d // 2
    last = planes + 1
    low, high = TOP, TOP + lines
    density = 3.0 / (planes * slabs)
    body_rows = slice(low, high)

    loads = [
        pltpu.make_async_copy(src, dst, load_sem.at[i])
        for i, (src, dst) in enumerate(
            [
                (k_in, kb.at[1:last, body_rows, :]),
                (f_in, fb.at[1:last, body_rows, :]),
                (r_in, rb),
            ]
        )
    ]
    for copy in loads:
        copy.start()

    barrier = pltpu.get_barrier_semaphore()
    x, z = chip // RING, lax.rem(chip, RING)
    lanes_x = chips // RING

    def along_z(step):
        return (x * RING + lax.rem(z + step, RING)) * 2 + core

    def along_x(step):
        return (lax.rem(x + step, lanes_x) * RING + z) * 2 + core

    z_next, z_prev = along_z(1), along_z(RING - 1)
    x_next, x_prev = along_x(1), along_x(lanes_x - 1)
    for other in (lax.rem(d + 1, slabs), lax.rem(d + slabs - 1, slabs), z_next, z_prev, x_next, x_prev):
        pl.semaphore_signal(barrier, inc=1, device_id={"depth": other})
    for other in (lax.rem(y + 1, bands), lax.rem(y + bands - 1, bands)):
        pl.semaphore_signal(barrier, inc=1, device_id={"rows": other})

    z_rounds = RING // 2 - 1
    rounds = z_rounds + lanes_x // 2

    def tell(n):
        after, before = (z_next, z_prev) if n < z_rounds else (x_next, x_prev)
        pl.semaphore_signal(known.at[n, 0], inc=1, device_id={"depth": after})
        pl.semaphore_signal(known.at[n, 1], inc=1, device_id={"depth": before})

    def hear(n):
        pl.semaphore_wait(known.at[n, 0], 1)
        pl.semaphore_wait(known.at[n, 1], 1)

    def clear_planes(plane):
        for buf in (fb, kb, ub, sb):
            buf[plane, body_rows, :] = jnp.zeros((lines, columns), jnp.float32)

    def clear_rows(row):
        for buf in (fb, kb, ub, sb):
            buf[1:last, row : row + 1, :] = jnp.zeros((planes, 1, columns), jnp.float32)

    pl.when(d == 0)(lambda: clear_planes(0))
    pl.when(d == slabs - 1)(lambda: clear_planes(last))
    pl.when(y == 0)(lambda: clear_rows(low - 1))
    pl.when(y == bands - 1)(lambda: clear_rows(high))
    pl.semaphore_wait(barrier, 8)

    def to_front(src, dst, n):
        return pltpu.make_async_remote_copy(
            src, dst.at[last, body_rows, :], face_send.at[n, 0], face_recv.at[n, 0], device_id={"depth": d - 1}
        )

    def to_back(src, dst, n):
        return pltpu.make_async_remote_copy(
            src, dst.at[0, body_rows, :], face_send.at[n, 1], face_recv.at[n, 1], device_id={"depth": d + 1}
        )

    def to_above(src, dst, a, b, n):
        return pltpu.make_async_remote_copy(
            src, dst.at[a:b, high : high + 1, :], row_send.at[n, 0], row_recv.at[n, 0], device_id={"rows": y - 1}
        )

    def to_below(src, dst, a, b, n):
        return pltpu.make_async_remote_copy(
            src, dst.at[a:b, low - 1 : low, :], row_send.at[n, 1], row_recv.at[n, 1], device_id={"rows": y + 1}
        )

    def face_copies(buf, n, src=None):
        first = buf.at[1, body_rows, :] if src is None else src.at[0]
        final = buf.at[planes, body_rows, :] if src is None else src.at[planes - 1]
        return to_front(first, buf, n), to_back(final, buf, n)

    def row_copies(buf, a, b, n, src=None):
        first = buf.at[a:b, low : low + 1, :] if src is None else src.at[:, 0:1, :]
        final = buf.at[a:b, high - 1 : high, :] if src is None else src.at[:, lines - 1 : lines, :]
        return to_above(first, buf, a, b, n), to_below(final, buf, a, b, n)

    def start_faces(copies):
        pl.when(d > 0)(lambda: copies[0].start())
        pl.when(d < slabs - 1)(lambda: copies[1].start())

    def start_rows(copies):
        pl.when(y > 0)(lambda: copies[0].start())
        pl.when(y < bands - 1)(lambda: copies[1].start())

    def arrive_faces(copies):
        pl.when(d < slabs - 1)(lambda: copies[0].wait_recv())
        pl.when(d > 0)(lambda: copies[1].wait_recv())

    def arrive_rows(copies):
        pl.when(y < bands - 1)(lambda: copies[0].wait_recv())
        pl.when(y > 0)(lambda: copies[1].wait_recv())

    def sent_faces(copies):
        pl.when(d > 0)(lambda: copies[0].wait_send())
        pl.when(d < slabs - 1)(lambda: copies[1].wait_send())

    def sent_rows(copies):
        pl.when(y > 0)(lambda: copies[0].wait_send())
        pl.when(y < bands - 1)(lambda: copies[1].wait_send())

    faces = [face_copies(fb, 0, f_in), face_copies(kb, 1, k_in), face_copies(ub, 2), face_copies(sb, 3)]
    rows = [
        row_copies(fb, 1, last, 0, f_in),
        row_copies(kb, 1, last, 1, k_in),
        row_copies(ub, 2, planes, 2),
        row_copies(ub, 1, 2, 3),
        row_copies(ub, planes, last, 4),
        row_copies(sb, 2, planes, 5),
        row_copies(sb, 1, 2, 6),
        row_copies(sb, planes, last, 7),
    ]
    start_faces(faces[0])
    start_faces(faces[1])
    start_rows(rows[0])
    start_rows(rows[1])
    tell(0)

    lane = lax.broadcasted_iota(jnp.int32, (BLOCK, columns), 1)
    row = lax.broadcasted_iota(jnp.int32, (BLOCK, columns), 0)
    at_start, at_end = lane == 0, lane == columns - 1
    at_top, at_bottom = row == 0, row == BLOCK - 1
    blocks = [low + BLOCK * i for i in range(lines // BLOCK)]
    edge_blocks, mid_blocks = (blocks[0], blocks[-1]), tuple(blocks[1:-1])

    def lower(ref, p, r):
        if r == blocks[-1]:
            v = ref[p, r : r + BLOCK, :]
            return jnp.where(at_bottom, v, pltpu.roll(v, BLOCK - 1, 0))
        return ref[p, r + 1 : r + 1 + BLOCK, :]

    loads[0].wait()

    def prepare(p, carry):
        for r in blocks:
            local = slice(r - low, r - low + BLOCK)
            k = kb[p + 1, r : r + BLOCK, :]
            ax[p, local, :] = k + jnp.where(at_end, 0.0, pltpu.roll(k, columns - 1, 1))
            ay[p, r : r + BLOCK, :] = k + lower(kb, p + 1, r)
            sg[p, local, :] = 0.5 + 0.5 * jnp.tanh(2.0 * k - 1.0)
        return carry

    lax.fori_loop(0, planes, prepare, 0)
    hear(0)
    tell(1)
    loads[1].wait()
    loads[2].wait()

    def react(src, dst, p, front=True, back=True):
        for r in blocks:
            here = slice(r, r + BLOCK)
            local = slice(r - low, r - low + BLOCK)
            u = src[p + 1, here, :]
            k = kb[p + 1, here, :]
            right = jnp.where(at_end, 0.0, pltpu.roll(u, columns - 1, 1))
            out = ax[p, local, :] * (right - u)
            flux = out - jnp.where(at_start, k * u, pltpu.roll(out, 1, 1))
            if front:
                flux = flux + (k + kb[p, here, :]) * (src[p, here, :] - u)
            if back:
                flux = flux + (k + kb[p + 2, here, :]) * (src[p + 2, here, :] - u)
            flux = flux + ay[p, here, :] * (lower(src, p + 1, r) - u)
            if r == low:
                above = jnp.where(at_top, u, pltpu.roll(u, 1, 0))
                flux = flux + (k + jnp.where(at_top, k, pltpu.roll(k, 1, 0))) * (above - u)
            else:
                flux = flux + ay[p, r - 1 : r - 1 + BLOCK, :] * (src[p + 1, r - 1 : r - 1 + BLOCK, :] - u)
            rate = STEP * rb[p, local, :]
            dst[p + 1, here, :] = u + (0.5 * STEP) * flux + rate * (jnp.tanh(u) - 0.5 * u)

    def react_all(src, dst):
        over(*inner, lambda p: react(src, dst, p))
        react(src, dst, 0, front=False)
        react(src, dst, planes - 1, back=False)

    def add_rows(src, dst, p):
        for edge, outside in ((low, low - 1), (high - 1, high)):
            edge, outside = slice(edge, edge + 1), slice(outside, outside + 1)
            face = kb[p + 1, edge, :] + kb[p + 1, outside, :]
            dst[p + 1, edge, :] += (0.5 * STEP) * face * (src[p + 1, outside, :] - src[p + 1, edge, :])

    def add_faces(src, dst):
        for edge, outside in ((1, 0), (planes, last)):
            for r in blocks:
                here = slice(r, r + BLOCK)
                face = kb[edge, here, :] + kb[outside, here, :]
                dst[edge, here, :] += (0.5 * STEP) * face * (src[outside, here, :] - src[edge, here, :])

    def over(start, count, stride, body):
        def lap(i, carry):
            body(start + stride * i)
            return carry

        lax.fori_loop(0, count, lap, 0)

    inner = (1, planes - 2, 1)
    outer = (0, 2, planes - 1)

    react_all(fb, ub)
    arrive_rows(rows[0])
    arrive_rows(rows[1])
    over(*inner, lambda p: add_rows(fb, ub, p))
    start_rows(rows[2])
    hear(1)
    tell(2)
    over(*outer, lambda p: add_rows(fb, ub, p))
    arrive_faces(faces[0])
    arrive_faces(faces[1])
    add_faces(fb, ub)
    start_faces(faces[2])
    start_rows(rows[3])
    start_rows(rows[4])
    hear(2)
    tell(3)

    react_all(ub, sb)
    arrive_rows(rows[2])
    over(*inner, lambda p: add_rows(ub, sb, p))
    start_rows(rows[5])
    hear(3)
    tell(4)
    arrive_rows(rows[3])
    arrive_rows(rows[4])
    over(*outer, lambda p: add_rows(ub, sb, p))
    arrive_faces(faces[2])
    add_faces(ub, sb)
    start_faces(faces[3])
    start_rows(rows[6])
    start_rows(rows[7])
    store = pltpu.make_async_copy(sb.at[1:last, body_rows, :], stepped, load_sem.at[3])
    store.start()

    def lit(g_depth, g_row, g_col):
        norm = g_depth * g_depth + g_row * g_row + g_col * g_col
        facing = jnp.abs(0.36 * g_depth + 0.45 * g_row + 0.48 * g_col)
        return 0.25 + facing * lax.rsqrt(jnp.maximum(norm, 4.0))

    def across(p, r):
        u = sb[p + 1, r : r + BLOCK, :]
        right = jnp.where(at_end, 0.0, pltpu.roll(u, columns - 1, 1))
        return right - jnp.where(at_start, 0.0, pltpu.roll(u, 1, 1))

    def matter(p, r):
        rise = jnp.exp(2.0 * sb[p + 1, r : r + BLOCK, :])
        whole = 1.0 + rise
        passed = jnp.exp(-density * jnp.log(whole))
        opacity = 1.0 - passed
        return opacity, opacity * (rise / whole), opacity * sg[p, r - low : r - low + BLOCK, :], passed

    def shade(p, r):
        here = slice(r, r + BLOCK)
        g_depth = sb[p + 2, here, :] - sb[p, here, :]
        g_row = sb[p + 1, r + 1 : r + 1 + BLOCK, :] - sb[p + 1, r - 1 : r - 1 + BLOCK, :]
        light = lit(g_depth, g_row, across(p, r))
        opacity, red, green, passed = matter(p, r)
        red = light * red
        return red, light * green, light * opacity - red, passed

    def shade_inner(p, some):
        for r in some:
            local = slice(r - low, r - low + BLOCK)
            through = acc[3, local, :]
            red, green, blue, passed = shade(p, r)
            acc[0, local, :] += through * red
            acc[1, local, :] += through * green
            acc[2, local, :] += through * blue
            acc[3, local, :] = through * passed

    acc[0:3] = jnp.zeros((3, lines, columns), jnp.float32)
    acc[3] = jnp.ones((lines, columns), jnp.float32)
    over(*inner, lambda p: shade_inner(p, mid_blocks))

    for r in blocks:
        local = slice(r - low, r - low + BLOCK)
        for q, p in enumerate((0, planes - 1)):
            gc[q, local, :] = across(p, r)
            opacity, red, green, passed = matter(p, r)
            ends[q, 0, local, :] = red
            ends[q, 1, local, :] = green
            ends[q, 2, local, :] = opacity - red
            ends[q, 3, local, :] = passed

    arrive_rows(rows[5])
    over(*inner, lambda p: shade_inner(p, edge_blocks))
    for r in blocks:
        local = slice(r - low, r - low + BLOCK)
        passed = ends[0, 3, local, :]
        through = passed * acc[3, local, :]
        for i in range(3):
            acc[i, local, :] = passed * acc[i, local, :]
            ends[1, i, local, :] = through * ends[1, i, local, :]
        acc[3, local, :] = through * ends[1, 3, local, :]

    partner = {"depth": chip * 2 + 1 - core}

    def pair_copy(t):
        part = pl.ds(t * per_tile, per_tile)
        return pltpu.make_async_remote_copy(
            pieces.at[part, 2], pieces.at[part, core], pair_send.at[t], pair_recv.at[t], device_id=partner
        )

    order = []
    for i in (lanes_x // 2, 1, lanes_x - 1, 0):
        for h in (1, 0):
            side = lax.rem(z // per_tile + h, 2)
            order.append(lax.rem(x + i, lanes_x) * 2 + side)

    def span(t):
        return pl.ds(pl.multiple_of(t * TILE, TILE), TILE)

    pass_copy = pltpu.make_async_remote_copy(
        front_pass.at[1], front_pass.at[1], pass_sem.at[0], pass_sem.at[1], device_id=partner
    )

    @pl.when(core == 0)
    def _():
        for t in range(tiles):
            stack = jnp.concatenate([acc[3, :, t * TILE : (t + 1) * TILE]] * 4, axis=0)
            turned = stack.T.reshape(per_tile, 2, width, 4 * lines)
            part = slice(t * per_tile, (t + 1) * per_tile)
            front_pass[0, part] = turned[:, 0]
            front_pass[1, part] = turned[:, 1]
        pass_copy.start()

    arrive_faces(faces[3])
    arrive_rows(rows[6])
    arrive_rows(rows[7])

    def light_of(p, q, cols):
        g_depth = sb[p + 2, body_rows, cols] - sb[p, body_rows, cols]
        g_row = sb[p + 1, low + 1 : high + 1, cols] - sb[p + 1, low - 1 : high - 1, cols]
        return lit(g_depth, g_row, gc[q, :, cols])

    for t in order:
        cols = span(t)
        first = light_of(0, 0, cols)
        final = light_of(planes - 1, 1, cols)
        stack = [acc[c, :, cols] + first * ends[0, c, :, cols] + final * ends[1, c, :, cols] for c in range(3)]
        stack = jnp.concatenate(stack + [acc[3, :, cols]], axis=0)
        turned = stack.T.reshape(per_tile, 2, width, 4 * lines)
        part = pl.ds(t * per_tile, per_tile)
        pieces[part, 2 * core] = turned[:, 0]
        pieces[part, 2 - core] = turned[:, 1]
        pair_copy(t).start()

    small = lax.broadcasted_iota(jnp.int32, (width, 4 * lines), 1)
    colour_lane = small < 3 * lines

    def spread(x):
        half = jnp.where(small >= 3 * lines, x, pltpu.roll(x, 3 * lines, 1))
        return jnp.where(small >= 2 * lines, half, pltpu.roll(half, 2 * lines, 1))

    def part_copy(to, slot):
        return pltpu.make_async_remote_copy(
            comb.at[to], seg.at[slot], part_send.at[0], part_recv.at[0], device_id={"depth": to * 2 + core}
        )

    def all_parts():
        others = pl.ds(0, chips - 1)
        return pltpu.make_async_remote_copy(
            comb.at[others], seg.at[others], part_send.at[0], part_recv.at[0], device_id={"depth": d}
        )

    hear(rounds - 1)
    pl.when(core == 1)(lambda: pass_copy.wait_recv())
    for t in order:
        pair_copy(t).wait_recv()
        for q in range(per_tile):
            m = t * per_tile + q
            front = pieces[m, 0]
            comb[m] = front_pass[core, m] * pieces[m, 1] + jnp.where(colour_lane, front, 0.0)
        for q in range(per_tile):
            m = t * per_tile + q
            pl.when(m != chip)(lambda: part_copy(m, chip).start())
    seg[chip] = comb[chip]

    shape = (width, 4 * lines)
    all_parts().wait_recv()
    total, through = jnp.zeros(shape, jnp.float32), jnp.ones(shape, jnp.float32)
    for m in range(chips):
        piece = seg[m]
        total = total + through * piece
        through = through * spread(piece)
    result = jnp.where(colour_lane, total, 1.0 - through)
    for c in range(4):
        image[c] = result[:, c * lines : (c + 1) * lines]

    all_parts().wait_send()

    def finish_pairs(t, carry):
        pair_copy(t).wait_send()
        return carry

    lax.fori_loop(0, tiles, finish_pairs, 0)
    pl.when(core == 0)(lambda: pass_copy.wait_send())
    for copies in faces:
        sent_faces(copies)
    for copies in rows:
        sent_rows(copies)
    store.wait()


def on_device(slabs, bands, field, coefficient, rate):
    planes, lines, columns = field.shape
    chips = slabs // 2
    width = columns // slabs
    padded = pltpu.VMEM((planes + 2, lines + 2 * TOP, columns), jnp.float32)
    plain = pltpu.VMEM((planes, lines, columns), jnp.float32)
    parts = pltpu.VMEM((chips, width, 4 * lines), jnp.float32)
    dma = pltpu.SemaphoreType.DMA
    stepped, image = pl.pallas_call(
        functools.partial(kernel, slabs, bands),
        out_shape=(
            jax.ShapeDtypeStruct(field.shape, jnp.float32),
            jax.ShapeDtypeStruct((4, width, lines), jnp.float32),
        ),
        in_specs=[pl.BlockSpec(memory_space=pltpu.HBM)] * 3,
        out_specs=(pl.BlockSpec(memory_space=pl.ANY), pl.BlockSpec(memory_space=pltpu.VMEM)),
        scratch_shapes=[
            padded,
            padded,
            plain,
            padded,
            padded,
            plain,
            pltpu.VMEM((planes, lines + 2 * TOP, columns), jnp.float32),
            plain,
            pltpu.VMEM((4, lines, columns), jnp.float32),
            pltpu.VMEM((2, lines, columns), jnp.float32),
            pltpu.VMEM((2, 4, lines, columns), jnp.float32),
            pltpu.VMEM((chips, 3, width, 4 * lines), jnp.float32),
            pltpu.VMEM((2, chips, width, 4 * lines), jnp.float32),
            parts,
            parts,
            dma((4,)),
            dma((4, 2)),
            dma((4, 2)),
            dma((8, 2)),
            dma((8, 2)),
            dma((columns // TILE,)),
            dma((columns // TILE,)),
            dma((1,)),
            dma((1,)),
            dma((2,)),
            pltpu.SemaphoreType.REGULAR((chips // RING // 2 + RING // 2 - 1, 2)),
        ],
        compiler_params=pltpu.CompilerParams(collective_id=0, has_side_effects=True, vmem_limit_bytes=40 << 20),
    )(*(pltpu.with_memory_space_constraint(v, pltpu.HBM) for v in (field, coefficient, rate)))
    return stepped, jnp.swapaxes(image, 1, 2)


def solution(mesh):
    return jax.shard_map(
        functools.partial(on_device, mesh.shape["depth"], mesh.shape["rows"]),
        mesh=mesh,
        in_specs=(P("depth", "rows", None),) * 3,
        out_specs=(P("depth", "rows", None), P(None, "rows", "depth")),
        check_vma=False,
    )
```

```python
import functools

import jax
import jax.numpy as jnp
from jax import lax
from jax.experimental import pallas as pl
from jax.experimental.pallas import tpu as pltpu
from jax.sharding import PartitionSpec as P

STEP = 0.15
TOP = 8
TILE = 128
BLOCK = 8
CHUNKS = 2
RING = 8


def kernel(
    slabs,
    bands,
    f_in,
    k_in,
    r_in,
    stepped,
    seg,
    fb,
    kb,
    rb,
    ub,
    sb,
    ax,
    ay,
    sg,
    acc,
    gc,
    ends,
    pieces,
    front_pass,
    comb,
    load_sem,
    face_send,
    face_recv,
    row_send,
    row_recv,
    pair_send,
    pair_recv,
    part_send,
    part_recv,
    pass_sem,
    known,
):
    d = lax.axis_index("depth")
    y = lax.axis_index("rows")
    planes, lines, columns = f_in.shape
    chips = slabs // 2
    width = columns // slabs
    tiles = columns // TILE
    per_tile = chips // tiles
    core = lax.rem(d, 2)
    chip = d // 2
    last = planes + 1
    low, high = TOP, TOP + lines
    density = 3.0 / (planes * slabs)
    body_rows = slice(low, high)
    spans = [slice(i * columns // CHUNKS, (i + 1) * columns // CHUNKS) for i in range(CHUNKS)]
    whole_span = slice(0, columns)

    loads = [
        pltpu.make_async_copy(src, dst, load_sem.at[i])
        for i, (src, dst) in enumerate(
            [
                (k_in, kb.at[1:last, body_rows, :]),
                (f_in, fb.at[1:last, body_rows, :]),
                (r_in, rb),
            ]
        )
    ]
    for copy in loads:
        copy.start()

    barrier = pltpu.get_barrier_semaphore()
    x, z = chip // RING, lax.rem(chip, RING)
    lanes_x = chips // RING

    def along_z(step):
        return (x * RING + lax.rem(z + step, RING)) * 2 + core

    def along_x(step):
        return (lax.rem(x + step, lanes_x) * RING + z) * 2 + core

    z_next, z_prev = along_z(1), along_z(RING - 1)
    x_next, x_prev = along_x(1), along_x(lanes_x - 1)
    for other in (lax.rem(d + 1, slabs), lax.rem(d + slabs - 1, slabs), z_next, z_prev, x_next, x_prev):
        pl.semaphore_signal(barrier, inc=1, device_id={"depth": other})
    for other in (lax.rem(y + 1, bands), lax.rem(y + bands - 1, bands)):
        pl.semaphore_signal(barrier, inc=1, device_id={"rows": other})

    z_rounds = RING // 2 - 1
    rounds = z_rounds + lanes_x // 2

    def tell(n):
        after, before = (z_next, z_prev) if n < z_rounds else (x_next, x_prev)
        pl.semaphore_signal(known.at[n, 0], inc=1, device_id={"depth": after})
        pl.semaphore_signal(known.at[n, 1], inc=1, device_id={"depth": before})

    def hear(n):
        pl.semaphore_wait(known.at[n, 0], 1)
        pl.semaphore_wait(known.at[n, 1], 1)

    def clear_planes(plane):
        for buf in (fb, kb, ub, sb):
            buf[plane, body_rows, :] = jnp.zeros((lines, columns), jnp.float32)

    def clear_rows(row):
        for buf in (fb, kb, ub, sb):
            buf[1:last, row : row + 1, :] = jnp.zeros((planes, 1, columns), jnp.float32)

    pl.when(d == 0)(lambda: clear_planes(0))
    pl.when(d == slabs - 1)(lambda: clear_planes(last))
    pl.when(y == 0)(lambda: clear_rows(low - 1))
    pl.when(y == bands - 1)(lambda: clear_rows(high))
    pl.semaphore_wait(barrier, 8)

    def to_front(src, dst, n, c):
        return pltpu.make_async_remote_copy(
            src, dst.at[last, body_rows, spans[c]], face_send.at[n, 0, c], face_recv.at[n, 0, c], device_id={"depth": d - 1}
        )

    def to_back(src, dst, n, c):
        return pltpu.make_async_remote_copy(
            src, dst.at[0, body_rows, spans[c]], face_send.at[n, 1, c], face_recv.at[n, 1, c], device_id={"depth": d + 1}
        )

    def to_above(src, dst, n, c):
        return pltpu.make_async_remote_copy(
            src, dst, row_send.at[n, 0, c], row_recv.at[n, 0, c], device_id={"rows": y - 1}
        )

    def to_below(src, dst, n, c):
        return pltpu.make_async_remote_copy(
            src, dst, row_send.at[n, 1, c], row_recv.at[n, 1, c], device_id={"rows": y + 1}
        )

    def face_copies(buf, n, c, src=None):
        first = buf.at[1, body_rows, spans[c]] if src is None else src.at[0, :, spans[c]]
        final = buf.at[planes, body_rows, spans[c]] if src is None else src.at[planes - 1, :, spans[c]]
        return to_front(first, buf, n, c), to_back(final, buf, n, c)

    def row_copies(buf, a, b, n, src=None, c=0, span=whole_span):
        first = buf.at[a:b, low : low + 1, span] if src is None else src.at[:, 0:1, span]
        final = buf.at[a:b, high - 1 : high, span] if src is None else src.at[:, lines - 1 : lines, span]
        return (
            to_above(first, buf.at[a:b, high : high + 1, span], n, c),
            to_below(final, buf.at[a:b, low - 1 : low, span], n, c),
        )

    def start_faces(copies):
        pl.when(d > 0)(lambda: copies[0].start())
        pl.when(d < slabs - 1)(lambda: copies[1].start())

    def start_rows(copies):
        pl.when(y > 0)(lambda: copies[0].start())
        pl.when(y < bands - 1)(lambda: copies[1].start())

    def arrive_faces(copies):
        pl.when(d < slabs - 1)(lambda: copies[0].wait_recv())
        pl.when(d > 0)(lambda: copies[1].wait_recv())

    def arrive_rows(copies):
        pl.when(y < bands - 1)(lambda: copies[0].wait_recv())
        pl.when(y > 0)(lambda: copies[1].wait_recv())

    def sent_faces(copies):
        pl.when(d > 0)(lambda: copies[0].wait_send())
        pl.when(d < slabs - 1)(lambda: copies[1].wait_send())

    def sent_rows(copies):
        pl.when(y > 0)(lambda: copies[0].wait_send())
        pl.when(y < bands - 1)(lambda: copies[1].wait_send())

    faces = [
        [face_copies(buf, n, c, src) for c in range(CHUNKS)]
        for n, (buf, src) in enumerate([(fb, f_in), (kb, k_in), (ub, None), (sb, None)])
    ]

    def end_rows(buf, n):
        return [
            [row_copies(buf, a, a + 1, n + i, None, c, spans[c]) for i, a in enumerate((1, planes))] for c in range(CHUNKS)
        ]

    rows = [
        row_copies(fb, 1, last, 0, f_in),
        row_copies(kb, 1, last, 1, k_in),
        row_copies(ub, 2, planes, 2),
        row_copies(sb, 2, planes, 5),
    ]
    u_ends, s_ends = end_rows(ub, 3), end_rows(sb, 6)
    for c in range(CHUNKS):
        start_faces(faces[0][c])
        start_faces(faces[1][c])
    start_rows(rows[0])
    start_rows(rows[1])
    tell(0)

    lane = lax.broadcasted_iota(jnp.int32, (BLOCK, columns), 1)
    row = lax.broadcasted_iota(jnp.int32, (BLOCK, columns), 0)
    at_start, at_end = lane == 0, lane == columns - 1
    at_top, at_bottom = row == 0, row == BLOCK - 1
    blocks = [low + BLOCK * i for i in range(lines // BLOCK)]
    edge_blocks, mid_blocks = (blocks[0], blocks[-1]), tuple(blocks[1:-1])

    def lower(ref, p, r):
        if r == blocks[-1]:
            v = ref[p, r : r + BLOCK, :]
            return jnp.where(at_bottom, v, pltpu.roll(v, BLOCK - 1, 0))
        return ref[p, r + 1 : r + 1 + BLOCK, :]

    loads[0].wait()

    def prepare(p, carry):
        for r in blocks:
            local = slice(r - low, r - low + BLOCK)
            k = kb[p + 1, r : r + BLOCK, :]
            ax[p, local, :] = k + jnp.where(at_end, 0.0, pltpu.roll(k, columns - 1, 1))
            ay[p, r : r + BLOCK, :] = k + lower(kb, p + 1, r)
            sg[p, local, :] = 0.5 + 0.5 * jnp.tanh(2.0 * k - 1.0)
        return carry

    lax.fori_loop(0, planes, prepare, 0)
    hear(0)
    tell(1)
    loads[1].wait()
    loads[2].wait()

    def react(src, dst, p, front=True, back=True):
        for r in blocks:
            here = slice(r, r + BLOCK)
            local = slice(r - low, r - low + BLOCK)
            u = src[p + 1, here, :]
            k = kb[p + 1, here, :]
            right = jnp.where(at_end, 0.0, pltpu.roll(u, columns - 1, 1))
            out = ax[p, local, :] * (right - u)
            flux = out - jnp.where(at_start, k * u, pltpu.roll(out, 1, 1))
            if front:
                flux = flux + (k + kb[p, here, :]) * (src[p, here, :] - u)
            if back:
                flux = flux + (k + kb[p + 2, here, :]) * (src[p + 2, here, :] - u)
            flux = flux + ay[p, here, :] * (lower(src, p + 1, r) - u)
            if r == low:
                above = jnp.where(at_top, u, pltpu.roll(u, 1, 0))
                flux = flux + (k + jnp.where(at_top, k, pltpu.roll(k, 1, 0))) * (above - u)
            else:
                flux = flux + ay[p, r - 1 : r - 1 + BLOCK, :] * (src[p + 1, r - 1 : r - 1 + BLOCK, :] - u)
            rate = STEP * rb[p, local, :]
            dst[p + 1, here, :] = u + (0.5 * STEP) * flux + rate * (jnp.tanh(u) - 0.5 * u)

    def react_all(src, dst):
        over(*inner, lambda p: react(src, dst, p))
        react(src, dst, 0, front=False)
        react(src, dst, planes - 1, back=False)

    def add_rows(src, dst, p, span=whole_span):
        for edge, outside in ((low, low - 1), (high - 1, high)):
            edge, outside = (slice(edge, edge + 1), span), (slice(outside, outside + 1), span)
            face = kb[p + 1, *edge] + kb[p + 1, *outside]
            dst[p + 1, *edge] += (0.5 * STEP) * face * (src[p + 1, *outside] - src[p + 1, *edge])

    def add_faces(src, dst, c):
        for edge, outside in ((1, 0), (planes, last)):
            for r in blocks:
                here = slice(r, r + BLOCK), spans[c]
                face = kb[edge, *here] + kb[outside, *here]
                dst[edge, *here] += (0.5 * STEP) * face * (src[outside, *here] - src[edge, *here])

    def over(start, count, stride, body):
        def lap(i, carry):
            body(start + stride * i)
            return carry

        lax.fori_loop(0, count, lap, 0)

    inner = (1, planes - 2, 1)
    outer = (0, 2, planes - 1)

    react_all(fb, ub)
    arrive_rows(rows[0])
    arrive_rows(rows[1])
    over(*inner, lambda p: add_rows(fb, ub, p))
    start_rows(rows[2])
    hear(1)
    tell(2)
    over(*outer, lambda p: add_rows(fb, ub, p))
    for c in range(CHUNKS):
        arrive_faces(faces[0][c])
        arrive_faces(faces[1][c])
        add_faces(fb, ub, c)
        start_faces(faces[2][c])
        for copies in u_ends[c]:
            start_rows(copies)
    hear(2)
    tell(3)

    react_all(ub, sb)
    arrive_rows(rows[2])
    over(*inner, lambda p: add_rows(ub, sb, p))
    start_rows(rows[3])
    hear(3)
    tell(4)
    for c in range(CHUNKS):
        for copies in u_ends[c]:
            arrive_rows(copies)
        over(*outer, lambda p: add_rows(ub, sb, p, spans[c]))
        arrive_faces(faces[2][c])
        add_faces(ub, sb, c)
        start_faces(faces[3][c])
        for copies in s_ends[c]:
            start_rows(copies)
    store = pltpu.make_async_copy(sb.at[1:last, body_rows, :], stepped, load_sem.at[3])
    store.start()

    def lit(g_depth, g_row, g_col):
        norm = g_depth * g_depth + g_row * g_row + g_col * g_col
        facing = jnp.abs(0.36 * g_depth + 0.45 * g_row + 0.48 * g_col)
        return 0.25 + facing * lax.rsqrt(jnp.maximum(norm, 4.0))

    def across(p, r):
        u = sb[p + 1, r : r + BLOCK, :]
        right = jnp.where(at_end, 0.0, pltpu.roll(u, columns - 1, 1))
        return right - jnp.where(at_start, 0.0, pltpu.roll(u, 1, 1))

    def matter(p, r):
        rise = jnp.exp(2.0 * sb[p + 1, r : r + BLOCK, :])
        whole = 1.0 + rise
        passed = jnp.exp(-density * jnp.log(whole))
        opacity = 1.0 - passed
        return opacity, opacity * (rise / whole), opacity * sg[p, r - low : r - low + BLOCK, :], passed

    def shade(p, r):
        here = slice(r, r + BLOCK)
        g_depth = sb[p + 2, here, :] - sb[p, here, :]
        g_row = sb[p + 1, r + 1 : r + 1 + BLOCK, :] - sb[p + 1, r - 1 : r - 1 + BLOCK, :]
        light = lit(g_depth, g_row, across(p, r))
        opacity, red, green, passed = matter(p, r)
        red = light * red
        return red, light * green, light * opacity - red, passed

    def shade_inner(p, some):
        for r in some:
            local = slice(r - low, r - low + BLOCK)
            through = acc[3, local, :]
            red, green, blue, passed = shade(p, r)
            acc[0, local, :] += through * red
            acc[1, local, :] += through * green
            acc[2, local, :] += through * blue
            acc[3, local, :] = through * passed

    acc[0:3] = jnp.zeros((3, lines, columns), jnp.float32)
    acc[3] = jnp.ones((lines, columns), jnp.float32)
    over(*inner, lambda p: shade_inner(p, mid_blocks))

    for r in blocks:
        local = slice(r - low, r - low + BLOCK)
        for q, p in enumerate((0, planes - 1)):
            gc[q, local, :] = across(p, r)
            opacity, red, green, passed = matter(p, r)
            ends[q, 0, local, :] = red
            ends[q, 1, local, :] = green
            ends[q, 2, local, :] = opacity - red
            ends[q, 3, local, :] = passed

    arrive_rows(rows[3])
    over(*inner, lambda p: shade_inner(p, edge_blocks))
    for r in blocks:
        local = slice(r - low, r - low + BLOCK)
        passed = ends[0, 3, local, :]
        through = passed * acc[3, local, :]
        for i in range(3):
            acc[i, local, :] = passed * acc[i, local, :]
            ends[1, i, local, :] = through * ends[1, i, local, :]
        acc[3, local, :] = through * ends[1, 3, local, :]

    partner = {"depth": chip * 2 + 1 - core}

    def pair_copy(t):
        part = pl.ds(t * per_tile, per_tile)
        return pltpu.make_async_remote_copy(
            pieces.at[part, 2], pieces.at[part, core], pair_send.at[t], pair_recv.at[t], device_id=partner
        )

    order = []
    for i in (lanes_x // 2, 1, lanes_x - 1, 0):
        for h in (1, 0):
            side = lax.rem(z // per_tile + h, 2)
            order.append(lax.rem(x + i, lanes_x) * 2 + side)

    def span(t):
        return pl.ds(pl.multiple_of(t * TILE, TILE), TILE)

    pass_copy = pltpu.make_async_remote_copy(
        front_pass.at[1], front_pass.at[1], pass_sem.at[0], pass_sem.at[1], device_id=partner
    )

    @pl.when(core == 0)
    def _():
        for t in range(tiles):
            stack = jnp.concatenate([acc[3, :, t * TILE : (t + 1) * TILE]] * 4, axis=0)
            turned = stack.T.reshape(per_tile, 2, width, 4 * lines)
            part = slice(t * per_tile, (t + 1) * per_tile)
            front_pass[0, part] = turned[:, 0]
            front_pass[1, part] = turned[:, 1]
        pass_copy.start()

    for c in range(CHUNKS):
        arrive_faces(faces[3][c])
        for copies in s_ends[c]:
            arrive_rows(copies)

    def light_of(p, q, cols):
        g_depth = sb[p + 2, body_rows, cols] - sb[p, body_rows, cols]
        g_row = sb[p + 1, low + 1 : high + 1, cols] - sb[p + 1, low - 1 : high - 1, cols]
        return lit(g_depth, g_row, gc[q, :, cols])

    for t in order:
        cols = span(t)
        first = light_of(0, 0, cols)
        final = light_of(planes - 1, 1, cols)
        stack = [acc[c, :, cols] + first * ends[0, c, :, cols] + final * ends[1, c, :, cols] for c in range(3)]
        stack = jnp.concatenate(stack + [acc[3, :, cols]], axis=0)
        turned = stack.T.reshape(per_tile, 2, width, 4 * lines)
        part = pl.ds(t * per_tile, per_tile)
        pieces[part, 2 * core] = turned[:, 0]
        pieces[part, 2 - core] = turned[:, 1]
        pair_copy(t).start()

    colour_lane = lax.broadcasted_iota(jnp.int32, (width, 4 * lines), 1) < 3 * lines

    def part_copy(to, slot):
        return pltpu.make_async_remote_copy(
            comb.at[to], seg.at[slot], part_send.at[0], part_recv.at[0], device_id={"depth": to * 2 + core}
        )

    def all_parts():
        others = pl.ds(0, chips - 1)
        return pltpu.make_async_remote_copy(
            comb.at[others], seg.at[others], part_send.at[0], part_recv.at[0], device_id={"depth": d}
        )

    hear(rounds - 1)
    pl.when(core == 1)(lambda: pass_copy.wait_recv())
    for t in order:
        pair_copy(t).wait_recv()
        for q in range(per_tile):
            m = t * per_tile + q
            front = pieces[m, 0]
            comb[m] = front_pass[core, m] * pieces[m, 1] + jnp.where(colour_lane, front, 0.0)
        for q in range(per_tile):
            m = t * per_tile + q
            pl.when(m != chip)(lambda: part_copy(m, chip).start())
    seg[chip] = comb[chip]

    all_parts().wait_recv()
    all_parts().wait_send()

    def finish_pairs(t, carry):
        pair_copy(t).wait_send()
        return carry

    lax.fori_loop(0, tiles, finish_pairs, 0)
    pl.when(core == 0)(lambda: pass_copy.wait_send())
    for copies in sum(faces, []):
        sent_faces(copies)
    for copies in rows + sum(u_ends + s_ends, []):
        sent_rows(copies)
    store.wait()


def finish(near, parts, stepped, image, picture, sems):
    chips, width, wide = parts.shape
    lines = wide // 4
    field_copy = pltpu.make_async_copy(near, stepped, sems.at[0])
    field_copy.start()
    lane = lax.broadcasted_iota(jnp.int32, (width, wide), 1)
    total, through = jnp.zeros((width, wide), jnp.float32), jnp.ones((width, wide), jnp.float32)
    for m in range(chips):
        piece = parts[m]
        total = total + through * piece
        half = jnp.where(lane >= 3 * lines, piece, pltpu.roll(piece, 3 * lines, 1))
        through = through * jnp.where(lane >= 2 * lines, half, pltpu.roll(half, 2 * lines, 1))
    result = jnp.where(lane < 3 * lines, total, 1.0 - through)
    for c in range(4):
        picture[c] = result[:, c * lines : (c + 1) * lines]
    image_copy = pltpu.make_async_copy(picture, image, sems.at[1])
    image_copy.start()
    image_copy.wait()
    field_copy.wait()


def on_device(slabs, bands, field, coefficient, rate):
    planes, lines, columns = field.shape
    chips = slabs // 2
    width = columns // slabs
    padded = pltpu.VMEM((planes + 2, lines + 2 * TOP, columns), jnp.float32)
    plain = pltpu.VMEM((planes, lines, columns), jnp.float32)
    parts = pltpu.VMEM((chips, width, 4 * lines), jnp.float32)
    dma = pltpu.SemaphoreType.DMA
    near, gathered = pl.pallas_call(
        functools.partial(kernel, slabs, bands),
        out_shape=(
            jax.ShapeDtypeStruct(field.shape, jnp.float32),
            jax.ShapeDtypeStruct((chips, width, 4 * lines), jnp.float32),
        ),
        in_specs=[pl.BlockSpec(memory_space=pltpu.HBM)] * 3,
        out_specs=(pl.BlockSpec(memory_space=pl.ANY), pl.BlockSpec(memory_space=pltpu.VMEM)),
        scratch_shapes=[
            padded,
            padded,
            plain,
            padded,
            padded,
            plain,
            pltpu.VMEM((planes, lines + 2 * TOP, columns), jnp.float32),
            plain,
            pltpu.VMEM((4, lines, columns), jnp.float32),
            pltpu.VMEM((2, lines, columns), jnp.float32),
            pltpu.VMEM((2, 4, lines, columns), jnp.float32),
            pltpu.VMEM((chips, 3, width, 4 * lines), jnp.float32),
            pltpu.VMEM((2, chips, width, 4 * lines), jnp.float32),
            parts,
            dma((4,)),
            dma((4, 2, CHUNKS)),
            dma((4, 2, CHUNKS)),
            dma((8, 2, CHUNKS)),
            dma((8, 2, CHUNKS)),
            dma((columns // TILE,)),
            dma((columns // TILE,)),
            dma((1,)),
            dma((1,)),
            dma((2,)),
            pltpu.SemaphoreType.REGULAR((chips // RING // 2 + RING // 2 - 1, 2)),
        ],
        compiler_params=pltpu.CompilerParams(collective_id=0, has_side_effects=True, vmem_limit_bytes=40 << 20),
    )(*(pltpu.with_memory_space_constraint(v, pltpu.HBM) for v in (field, coefficient, rate)))
    stepped, image = pl.pallas_call(
        finish,
        out_shape=(
            jax.ShapeDtypeStruct(field.shape, jnp.float32),
            jax.ShapeDtypeStruct((4, width, lines), jnp.float32),
        ),
        in_specs=[pl.BlockSpec(memory_space=pl.ANY), pl.BlockSpec(memory_space=pltpu.VMEM)],
        out_specs=(pl.BlockSpec(memory_space=pltpu.HBM), pl.BlockSpec(memory_space=pltpu.HBM)),
        scratch_shapes=[pltpu.VMEM((4, width, lines), jnp.float32), dma((2,))],
        compiler_params=pltpu.CompilerParams(vmem_limit_bytes=8 << 20),
    )(near, gathered)
    return stepped, jnp.swapaxes(image, 1, 2)


def solution(mesh):
    return jax.shard_map(
        functools.partial(on_device, mesh.shape["depth"], mesh.shape["rows"]),
        mesh=mesh,
        in_specs=(P("depth", "rows", None),) * 3,
        out_specs=(P("depth", "rows", None), P(None, "rows", "depth")),
        check_vma=False,
    )
```

```python
import functools

import jax
import jax.numpy as jnp
from jax import lax
from jax.experimental import pallas as pl
from jax.experimental.pallas import tpu as pltpu
from jax.sharding import PartitionSpec as P

STEP = 0.15
TOP = 8
TILE = 128
BLOCK = 8
CHUNKS = 2
RING = 8


def kernel(
    slabs,
    bands,
    f_in,
    k_in,
    r_in,
    stepped,
    seg,
    fb,
    kb,
    rb,
    ub,
    sb,
    ax,
    ay,
    sg,
    acc,
    gc,
    ends,
    pieces,
    front_pass,
    comb,
    load_sem,
    face_send,
    face_recv,
    row_send,
    row_recv,
    pair_send,
    pair_recv,
    part_send,
    part_recv,
    pass_sem,
    known,
):
    d = lax.axis_index("depth")
    y = lax.axis_index("rows")
    planes, lines, columns = f_in.shape
    chips = slabs // 2
    width = columns // slabs
    tiles = columns // TILE
    per_tile = chips // tiles
    core = lax.rem(d, 2)
    chip = d // 2
    last = planes + 1
    low, high = TOP, TOP + lines
    density = 3.0 / (planes * slabs)
    body_rows = slice(low, high)
    spans = [slice(i * columns // CHUNKS, (i + 1) * columns // CHUNKS) for i in range(CHUNKS)]
    whole_span = slice(0, columns)

    loads = [
        pltpu.make_async_copy(src, dst, load_sem.at[i])
        for i, (src, dst) in enumerate(
            [
                (k_in, kb.at[1:last, body_rows, :]),
                (f_in, fb.at[1:last, body_rows, :]),
                (r_in, rb),
            ]
        )
    ]
    barrier = pltpu.get_barrier_semaphore()
    x, z = chip // RING, lax.rem(chip, RING)
    lanes_x = chips // RING

    def along_z(step):
        return (x * RING + lax.rem(z + step, RING)) * 2 + core

    def along_x(step):
        return (lax.rem(x + step, lanes_x) * RING + z) * 2 + core

    z_next, z_prev = along_z(1), along_z(RING - 1)
    x_next, x_prev = along_x(1), along_x(lanes_x - 1)
    for other in (lax.rem(d + 1, slabs), lax.rem(d + slabs - 1, slabs), z_next, z_prev, x_next, x_prev):
        pl.semaphore_signal(barrier, inc=1, device_id={"depth": other})
    for other in (lax.rem(y + 1, bands), lax.rem(y + bands - 1, bands)):
        pl.semaphore_signal(barrier, inc=1, device_id={"rows": other})

    for copy in loads:
        copy.start()

    z_rounds = RING // 2 - 1
    rounds = z_rounds + lanes_x // 2

    def tell(n):
        after, before = (z_next, z_prev) if n < z_rounds else (x_next, x_prev)
        pl.semaphore_signal(known.at[n, 0], inc=1, device_id={"depth": after})
        pl.semaphore_signal(known.at[n, 1], inc=1, device_id={"depth": before})

    def hear(n):
        pl.semaphore_wait(known.at[n, 0], 1)
        pl.semaphore_wait(known.at[n, 1], 1)

    def clear_planes(plane):
        for buf in (fb, kb, ub, sb):
            buf[plane, body_rows, :] = jnp.zeros((lines, columns), jnp.float32)

    def clear_rows(row):
        for buf in (fb, kb, ub, sb):
            buf[1:last, row : row + 1, :] = jnp.zeros((planes, 1, columns), jnp.float32)

    pl.when(d == 0)(lambda: clear_planes(0))
    pl.when(d == slabs - 1)(lambda: clear_planes(last))
    pl.when(y == 0)(lambda: clear_rows(low - 1))
    pl.when(y == bands - 1)(lambda: clear_rows(high))
    pl.semaphore_wait(barrier, 8)

    def to_front(src, dst, n, c):
        return pltpu.make_async_remote_copy(
            src, dst.at[last, body_rows, spans[c]], face_send.at[n, 0, c], face_recv.at[n, 0, c], device_id={"depth": d - 1}
        )

    def to_back(src, dst, n, c):
        return pltpu.make_async_remote_copy(
            src, dst.at[0, body_rows, spans[c]], face_send.at[n, 1, c], face_recv.at[n, 1, c], device_id={"depth": d + 1}
        )

    def to_above(src, dst, n, c):
        return pltpu.make_async_remote_copy(
            src, dst, row_send.at[n, 0, c], row_recv.at[n, 0, c], device_id={"rows": y - 1}
        )

    def to_below(src, dst, n, c):
        return pltpu.make_async_remote_copy(
            src, dst, row_send.at[n, 1, c], row_recv.at[n, 1, c], device_id={"rows": y + 1}
        )

    def face_copies(buf, n, c, src=None):
        first = buf.at[1, body_rows, spans[c]] if src is None else src.at[0, :, spans[c]]
        final = buf.at[planes, body_rows, spans[c]] if src is None else src.at[planes - 1, :, spans[c]]
        return to_front(first, buf, n, c), to_back(final, buf, n, c)

    def row_copies(buf, a, b, n, src=None, c=0, span=whole_span):
        first = buf.at[a:b, low : low + 1, span] if src is None else src.at[:, 0:1, span]
        final = buf.at[a:b, high - 1 : high, span] if src is None else src.at[:, lines - 1 : lines, span]
        return (
            to_above(first, buf.at[a:b, high : high + 1, span], n, c),
            to_below(final, buf.at[a:b, low - 1 : low, span], n, c),
        )

    def start_faces(copies):
        pl.when(d > 0)(lambda: copies[0].start())
        pl.when(d < slabs - 1)(lambda: copies[1].start())

    def start_rows(copies):
        pl.when(y > 0)(lambda: copies[0].start())
        pl.when(y < bands - 1)(lambda: copies[1].start())

    def arrive_faces(copies):
        pl.when(d < slabs - 1)(lambda: copies[0].wait_recv())
        pl.when(d > 0)(lambda: copies[1].wait_recv())

    def arrive_rows(copies):
        pl.when(y < bands - 1)(lambda: copies[0].wait_recv())
        pl.when(y > 0)(lambda: copies[1].wait_recv())

    def sent_faces(copies):
        pl.when(d > 0)(lambda: copies[0].wait_send())
        pl.when(d < slabs - 1)(lambda: copies[1].wait_send())

    def sent_rows(copies):
        pl.when(y > 0)(lambda: copies[0].wait_send())
        pl.when(y < bands - 1)(lambda: copies[1].wait_send())

    faces = [
        [face_copies(buf, n, c, src) for c in range(CHUNKS)]
        for n, (buf, src) in enumerate([(fb, f_in), (kb, k_in), (ub, None), (sb, None)])
    ]

    def end_rows(buf, n):
        return [
            [row_copies(buf, a, a + 1, n + i, None, c, spans[c]) for i, a in enumerate((1, planes))] for c in range(CHUNKS)
        ]

    rows = [
        row_copies(fb, 1, last, 0, f_in),
        row_copies(kb, 1, last, 1, k_in),
        row_copies(ub, 2, planes, 2),
        row_copies(sb, 2, planes, 5),
    ]
    u_ends, s_ends = end_rows(ub, 3), end_rows(sb, 6)
    for c in range(CHUNKS):
        start_faces(faces[0][c])
        start_faces(faces[1][c])
    start_rows(rows[0])
    start_rows(rows[1])
    tell(0)

    lane = lax.broadcasted_iota(jnp.int32, (BLOCK, columns), 1)
    row = lax.broadcasted_iota(jnp.int32, (BLOCK, columns), 0)
    at_start, at_end = lane == 0, lane == columns - 1
    at_top, at_bottom = row == 0, row == BLOCK - 1
    blocks = [low + BLOCK * i for i in range(lines // BLOCK)]
    edge_blocks, mid_blocks = (blocks[0], blocks[-1]), tuple(blocks[1:-1])

    def lower(ref, p, r):
        if r == blocks[-1]:
            v = ref[p, r : r + BLOCK, :]
            return jnp.where(at_bottom, v, pltpu.roll(v, BLOCK - 1, 0))
        return ref[p, r + 1 : r + 1 + BLOCK, :]

    loads[0].wait()

    def prepare(p, carry):
        for r in blocks:
            local = slice(r - low, r - low + BLOCK)
            k = kb[p + 1, r : r + BLOCK, :]
            ax[p, local, :] = k + jnp.where(at_end, 0.0, pltpu.roll(k, columns - 1, 1))
            ay[p, r : r + BLOCK, :] = k + lower(kb, p + 1, r)
            sg[p, local, :] = 0.5 + 0.5 * jnp.tanh(2.0 * k - 1.0)
        return carry

    lax.fori_loop(0, planes, prepare, 0)
    hear(0)
    tell(1)
    loads[1].wait()
    loads[2].wait()

    def react(src, dst, p, front=True, back=True):
        for r in blocks:
            here = slice(r, r + BLOCK)
            local = slice(r - low, r - low + BLOCK)
            u = src[p + 1, here, :]
            k = kb[p + 1, here, :]
            right = jnp.where(at_end, 0.0, pltpu.roll(u, columns - 1, 1))
            out = ax[p, local, :] * (right - u)
            flux = out - jnp.where(at_start, k * u, pltpu.roll(out, 1, 1))
            if front:
                flux = flux + (k + kb[p, here, :]) * (src[p, here, :] - u)
            if back:
                flux = flux + (k + kb[p + 2, here, :]) * (src[p + 2, here, :] - u)
            flux = flux + ay[p, here, :] * (lower(src, p + 1, r) - u)
            if r == low:
                above = jnp.where(at_top, u, pltpu.roll(u, 1, 0))
                flux = flux + (k + jnp.where(at_top, k, pltpu.roll(k, 1, 0))) * (above - u)
            else:
                flux = flux + ay[p, r - 1 : r - 1 + BLOCK, :] * (src[p + 1, r - 1 : r - 1 + BLOCK, :] - u)
            rate = STEP * rb[p, local, :]
            dst[p + 1, here, :] = u + (0.5 * STEP) * flux + rate * (jnp.tanh(u) - 0.5 * u)

    def react_all(src, dst):
        over(*inner, lambda p: react(src, dst, p))
        react(src, dst, 0, front=False)
        react(src, dst, planes - 1, back=False)

    def add_rows(src, dst, p, span=whole_span):
        for edge, outside in ((low, low - 1), (high - 1, high)):
            edge, outside = (slice(edge, edge + 1), span), (slice(outside, outside + 1), span)
            face = kb[p + 1, *edge] + kb[p + 1, *outside]
            dst[p + 1, *edge] += (0.5 * STEP) * face * (src[p + 1, *outside] - src[p + 1, *edge])

    def add_faces(src, dst, c):
        for edge, outside in ((1, 0), (planes, last)):
            for r in blocks:
                here = slice(r, r + BLOCK), spans[c]
                face = kb[edge, *here] + kb[outside, *here]
                dst[edge, *here] += (0.5 * STEP) * face * (src[outside, *here] - src[edge, *here])

    def over(start, count, stride, body):
        def lap(i, carry):
            body(start + stride * i)
            return carry

        lax.fori_loop(0, count, lap, 0)

    inner = (1, planes - 2, 1)
    outer = (0, 2, planes - 1)

    react_all(fb, ub)
    arrive_rows(rows[0])
    arrive_rows(rows[1])
    over(*inner, lambda p: add_rows(fb, ub, p))
    start_rows(rows[2])
    hear(1)
    tell(2)
    over(*outer, lambda p: add_rows(fb, ub, p))
    for c in range(CHUNKS):
        arrive_faces(faces[0][c])
        arrive_faces(faces[1][c])
        add_faces(fb, ub, c)
        for copies in u_ends[c]:
            start_rows(copies)
        start_faces(faces[2][c])
    hear(2)
    tell(3)

    react_all(ub, sb)
    arrive_rows(rows[2])
    over(*inner, lambda p: add_rows(ub, sb, p))
    start_rows(rows[3])
    hear(3)
    tell(4)
    for c in range(CHUNKS):
        for copies in u_ends[c]:
            arrive_rows(copies)
        over(*outer, lambda p: add_rows(ub, sb, p, spans[c]))
        arrive_faces(faces[2][c])
        add_faces(ub, sb, c)
        for copies in s_ends[c]:
            start_rows(copies)
        start_faces(faces[3][c])
    store = pltpu.make_async_copy(sb.at[1:last, body_rows, :], stepped, load_sem.at[3])
    store.start()

    def lit(g_depth, g_row, g_col):
        norm = g_depth * g_depth + g_row * g_row + g_col * g_col
        facing = jnp.abs(0.36 * g_depth + 0.45 * g_row + 0.48 * g_col)
        return 0.25 + facing * lax.rsqrt(jnp.maximum(norm, 4.0))

    def across(p, r):
        u = sb[p + 1, r : r + BLOCK, :]
        right = jnp.where(at_end, 0.0, pltpu.roll(u, columns - 1, 1))
        return right - jnp.where(at_start, 0.0, pltpu.roll(u, 1, 1))

    def matter(p, r):
        rise = jnp.exp(2.0 * sb[p + 1, r : r + BLOCK, :])
        whole = 1.0 + rise
        passed = jnp.exp(-density * jnp.log(whole))
        opacity = 1.0 - passed
        return opacity, opacity * (rise / whole), opacity * sg[p, r - low : r - low + BLOCK, :], passed

    def shade(p, r):
        here = slice(r, r + BLOCK)
        g_depth = sb[p + 2, here, :] - sb[p, here, :]
        g_row = sb[p + 1, r + 1 : r + 1 + BLOCK, :] - sb[p + 1, r - 1 : r - 1 + BLOCK, :]
        light = lit(g_depth, g_row, across(p, r))
        opacity, red, green, passed = matter(p, r)
        red = light * red
        return red, light * green, light * opacity - red, passed

    def shade_inner(p, some):
        for r in some:
            local = slice(r - low, r - low + BLOCK)
            through = acc[3, local, :]
            red, green, blue, passed = shade(p, r)
            acc[0, local, :] += through * red
            acc[1, local, :] += through * green
            acc[2, local, :] += through * blue
            acc[3, local, :] = through * passed

    acc[0:3] = jnp.zeros((3, lines, columns), jnp.float32)
    acc[3] = jnp.ones((lines, columns), jnp.float32)
    over(*inner, lambda p: shade_inner(p, mid_blocks))

    for r in blocks:
        local = slice(r - low, r - low + BLOCK)
        for q, p in enumerate((0, planes - 1)):
            gc[q, local, :] = across(p, r)
            opacity, red, green, passed = matter(p, r)
            ends[q, 0, local, :] = red
            ends[q, 1, local, :] = green
            ends[q, 2, local, :] = opacity - red
            ends[q, 3, local, :] = passed

    arrive_rows(rows[3])
    over(*inner, lambda p: shade_inner(p, edge_blocks))
    for r in blocks:
        local = slice(r - low, r - low + BLOCK)
        passed = ends[0, 3, local, :]
        through = passed * acc[3, local, :]
        for i in range(3):
            acc[i, local, :] = passed * acc[i, local, :]
            ends[1, i, local, :] = through * ends[1, i, local, :]
        acc[3, local, :] = through * ends[1, 3, local, :]

    partner = {"depth": chip * 2 + 1 - core}

    def pair_copy(t):
        part = pl.ds(t * per_tile, per_tile)
        return pltpu.make_async_remote_copy(
            pieces.at[part, 2], pieces.at[part, core], pair_send.at[t], pair_recv.at[t], device_id=partner
        )

    order = []
    for i in (lanes_x // 2, 1, lanes_x - 1, 0):
        for h in (1, 0):
            side = lax.rem(z // per_tile + h, 2)
            order.append(lax.rem(x + i, lanes_x) * 2 + side)

    def span(t):
        return pl.ds(pl.multiple_of(t * TILE, TILE), TILE)

    pass_copy = pltpu.make_async_remote_copy(
        front_pass.at[1], front_pass.at[1], pass_sem.at[0], pass_sem.at[1], device_id=partner
    )

    @pl.when(core == 0)
    def _():
        for t in range(tiles):
            stack = jnp.concatenate([acc[3, :, t * TILE : (t + 1) * TILE]] * 4, axis=0)
            turned = stack.T.reshape(per_tile, 2, width, 4 * lines)
            part = slice(t * per_tile, (t + 1) * per_tile)
            front_pass[0, part] = turned[:, 0]
            front_pass[1, part] = turned[:, 1]
        pass_copy.start()

    for c in range(CHUNKS):
        arrive_faces(faces[3][c])
        for copies in s_ends[c]:
            arrive_rows(copies)

    def light_of(p, q, cols):
        g_depth = sb[p + 2, body_rows, cols] - sb[p, body_rows, cols]
        g_row = sb[p + 1, low + 1 : high + 1, cols] - sb[p + 1, low - 1 : high - 1, cols]
        return lit(g_depth, g_row, gc[q, :, cols])

    for t in order:
        cols = span(t)
        first = light_of(0, 0, cols)
        final = light_of(planes - 1, 1, cols)
        stack = [acc[c, :, cols] + first * ends[0, c, :, cols] + final * ends[1, c, :, cols] for c in range(3)]
        stack = jnp.concatenate(stack + [acc[3, :, cols]], axis=0)
        turned = stack.T.reshape(per_tile, 2, width, 4 * lines)
        part = pl.ds(t * per_tile, per_tile)
        pieces[part, 2 * core] = turned[:, 0]
        pieces[part, 2 - core] = turned[:, 1]
        pair_copy(t).start()

    colour_lane = lax.broadcasted_iota(jnp.int32, (width, 4 * lines), 1) < 3 * lines

    def part_copy(to, slot):
        return pltpu.make_async_remote_copy(
            comb.at[to], seg.at[slot], part_send.at[0], part_recv.at[0], device_id={"depth": to * 2 + core}
        )

    def all_parts():
        others = pl.ds(0, chips - 1)
        return pltpu.make_async_remote_copy(
            comb.at[others], seg.at[others], part_send.at[0], part_recv.at[0], device_id={"depth": d}
        )

    hear(rounds - 1)
    pl.when(core == 1)(lambda: pass_copy.wait_recv())
    for t in order:
        pair_copy(t).wait_recv()
        for q in range(per_tile):
            m = t * per_tile + q
            front = pieces[m, 0]
            comb[m] = front_pass[core, m] * pieces[m, 1] + jnp.where(colour_lane, front, 0.0)
        for q in range(per_tile):
            m = t * per_tile + q
            pl.when(m != chip)(lambda: part_copy(m, chip).start())
    seg[chip] = comb[chip]

    all_parts().wait_recv()
    all_parts().wait_send()

    def finish_pairs(t, carry):
        pair_copy(t).wait_send()
        return carry

    lax.fori_loop(0, tiles, finish_pairs, 0)
    pl.when(core == 0)(lambda: pass_copy.wait_send())
    for copies in sum(faces, []):
        sent_faces(copies)
    for copies in rows + sum(u_ends + s_ends, []):
        sent_rows(copies)
    store.wait()


def finish(near, parts, stepped, image, picture, sems):
    chips, width, wide = parts.shape
    lines = wide // 4
    field_copies = [pltpu.make_async_copy(near.at[p], stepped.at[p], sems.at[1 + p]) for p in range(near.shape[0])]
    for copy in field_copies:
        copy.start()
    lane = lax.broadcasted_iota(jnp.int32, (width, wide), 1)
    total, through = jnp.zeros((width, wide), jnp.float32), jnp.ones((width, wide), jnp.float32)
    for m in range(chips):
        piece = parts[m]
        total = total + through * piece
        half = jnp.where(lane >= 3 * lines, piece, pltpu.roll(piece, 3 * lines, 1))
        through = through * jnp.where(lane >= 2 * lines, half, pltpu.roll(half, 2 * lines, 1))
    result = jnp.where(lane < 3 * lines, total, 1.0 - through)
    for c in range(4):
        picture[c] = result[:, c * lines : (c + 1) * lines]
    image_copy = pltpu.make_async_copy(picture, image, sems.at[0])
    image_copy.start()
    image_copy.wait()
    for copy in field_copies:
        copy.wait()


def on_device(slabs, bands, field, coefficient, rate):
    planes, lines, columns = field.shape
    chips = slabs // 2
    width = columns // slabs
    padded = pltpu.VMEM((planes + 2, lines + 2 * TOP, columns), jnp.float32)
    plain = pltpu.VMEM((planes, lines, columns), jnp.float32)
    parts = pltpu.VMEM((chips, width, 4 * lines), jnp.float32)
    dma = pltpu.SemaphoreType.DMA
    near, gathered = pl.pallas_call(
        functools.partial(kernel, slabs, bands),
        out_shape=(
            jax.ShapeDtypeStruct(field.shape, jnp.float32),
            jax.ShapeDtypeStruct((chips, width, 4 * lines), jnp.float32),
        ),
        in_specs=[pl.BlockSpec(memory_space=pltpu.HBM)] * 3,
        out_specs=(pl.BlockSpec(memory_space=pl.ANY), pl.BlockSpec(memory_space=pltpu.VMEM)),
        scratch_shapes=[
            padded,
            padded,
            plain,
            padded,
            padded,
            plain,
            pltpu.VMEM((planes, lines + 2 * TOP, columns), jnp.float32),
            plain,
            pltpu.VMEM((4, lines, columns), jnp.float32),
            pltpu.VMEM((2, lines, columns), jnp.float32),
            pltpu.VMEM((2, 4, lines, columns), jnp.float32),
            pltpu.VMEM((chips, 3, width, 4 * lines), jnp.float32),
            pltpu.VMEM((2, chips, width, 4 * lines), jnp.float32),
            parts,
            dma((4,)),
            dma((4, 2, CHUNKS)),
            dma((4, 2, CHUNKS)),
            dma((8, 2, CHUNKS)),
            dma((8, 2, CHUNKS)),
            dma((columns // TILE,)),
            dma((columns // TILE,)),
            dma((1,)),
            dma((1,)),
            dma((2,)),
            pltpu.SemaphoreType.REGULAR((chips // RING // 2 + RING // 2 - 1, 2)),
        ],
        compiler_params=pltpu.CompilerParams(collective_id=0, has_side_effects=True, vmem_limit_bytes=40 << 20),
    )(*(pltpu.with_memory_space_constraint(v, pltpu.HBM) for v in (field, coefficient, rate)))
    stepped, image = pl.pallas_call(
        finish,
        out_shape=(
            jax.ShapeDtypeStruct(field.shape, jnp.float32),
            jax.ShapeDtypeStruct((4, width, lines), jnp.float32),
        ),
        in_specs=[pl.BlockSpec(memory_space=pl.ANY), pl.BlockSpec(memory_space=pltpu.VMEM)],
        out_specs=(pl.BlockSpec(memory_space=pltpu.HBM), pl.BlockSpec(memory_space=pltpu.HBM)),
        scratch_shapes=[pltpu.VMEM((4, width, lines), jnp.float32), dma((1 + planes,))],
        compiler_params=pltpu.CompilerParams(vmem_limit_bytes=8 << 20),
    )(near, gathered)
    return stepped, jnp.swapaxes(image, 1, 2)


def solution(mesh):
    return jax.shard_map(
        functools.partial(on_device, mesh.shape["depth"], mesh.shape["rows"]),
        mesh=mesh,
        in_specs=(P("depth", "rows", None),) * 3,
        out_specs=(P("depth", "rows", None), P(None, "rows", "depth")),
        check_vma=False,
    )
```

```python
import functools

import jax
import jax.numpy as jnp
from jax import lax
from jax.experimental import pallas as pl
from jax.experimental.pallas import tpu as pltpu
from jax.sharding import PartitionSpec as P

STEP = 0.15
TOP = 8
TILE = 128
BLOCK = 8
CHUNKS = 2
RING = 8


def kernel(
    slabs,
    bands,
    f_in,
    k_in,
    r_in,
    stepped,
    seg,
    fb,
    kb,
    rb,
    ub,
    sb,
    ax,
    ay,
    sg,
    acc,
    gc,
    ends,
    pieces,
    front_pass,
    comb,
    load_sem,
    face_send,
    face_recv,
    row_send,
    row_recv,
    pair_send,
    pair_recv,
    part_send,
    part_recv,
    pass_sem,
    known,
):
    d = lax.axis_index("depth")
    y = lax.axis_index("rows")
    planes, lines, columns = f_in.shape
    chips = slabs // 2
    width = columns // slabs
    tiles = columns // TILE
    per_tile = chips // tiles
    core = lax.rem(d, 2)
    chip = d // 2
    last = planes + 1
    low, high = TOP, TOP + lines
    density = 3.0 / (planes * slabs)
    body_rows = slice(low, high)
    spans = [slice(i * columns // CHUNKS, (i + 1) * columns // CHUNKS) for i in range(CHUNKS)]
    whole_span = slice(0, columns)

    loads = [
        pltpu.make_async_copy(src, dst, load_sem.at[i])
        for i, (src, dst) in enumerate(
            [
                (k_in, kb.at[1:last, body_rows, :]),
                (f_in, fb.at[1:last, body_rows, :]),
                (r_in, rb),
            ]
        )
    ]
    for copy in loads:
        copy.start()

    barrier = pltpu.get_barrier_semaphore()
    x, z = chip // RING, lax.rem(chip, RING)
    lanes_x = chips // RING

    def along_z(step):
        return (x * RING + lax.rem(z + step, RING)) * 2 + core

    def along_x(step):
        return (lax.rem(x + step, lanes_x) * RING + z) * 2 + core

    z_next, z_prev = along_z(1), along_z(RING - 1)
    x_next, x_prev = along_x(1), along_x(lanes_x - 1)
    for other in (lax.rem(d + 1, slabs), lax.rem(d + slabs - 1, slabs), z_next, z_prev, x_next, x_prev):
        pl.semaphore_signal(barrier, inc=1, device_id={"depth": other})
    for other in (lax.rem(y + 1, bands), lax.rem(y + bands - 1, bands)):
        pl.semaphore_signal(barrier, inc=1, device_id={"rows": other})

    z_rounds = RING // 2 - 1
    rounds = z_rounds + lanes_x // 2

    def tell(n):
        after, before = (z_next, z_prev) if n < z_rounds else (x_next, x_prev)
        pl.semaphore_signal(known.at[n, 0], inc=1, device_id={"depth": after})
        pl.semaphore_signal(known.at[n, 1], inc=1, device_id={"depth": before})

    def hear(n):
        pl.semaphore_wait(known.at[n, 0], 1)
        pl.semaphore_wait(known.at[n, 1], 1)

    def clear_planes(plane):
        for buf in (fb, kb, ub, sb):
            buf[plane, body_rows, :] = jnp.zeros((lines, columns), jnp.float32)

    def clear_rows(row):
        for buf in (fb, kb, ub, sb):
            buf[1:last, row : row + 1, :] = jnp.zeros((planes, 1, columns), jnp.float32)

    pl.when(d == 0)(lambda: clear_planes(0))
    pl.when(d == slabs - 1)(lambda: clear_planes(last))
    pl.when(y == 0)(lambda: clear_rows(low - 1))
    pl.when(y == bands - 1)(lambda: clear_rows(high))
    pl.semaphore_wait(barrier, 8)

    def to_front(src, dst, n, c):
        return pltpu.make_async_remote_copy(
            src, dst.at[last, body_rows, spans[c]], face_send.at[n, 0, c], face_recv.at[n, 0, c], device_id={"depth": d - 1}
        )

    def to_back(src, dst, n, c):
        return pltpu.make_async_remote_copy(
            src, dst.at[0, body_rows, spans[c]], face_send.at[n, 1, c], face_recv.at[n, 1, c], device_id={"depth": d + 1}
        )

    def to_above(src, dst, n, c):
        return pltpu.make_async_remote_copy(
            src, dst, row_send.at[n, 0, c], row_recv.at[n, 0, c], device_id={"rows": y - 1}
        )

    def to_below(src, dst, n, c):
        return pltpu.make_async_remote_copy(
            src, dst, row_send.at[n, 1, c], row_recv.at[n, 1, c], device_id={"rows": y + 1}
        )

    def face_copies(buf, n, c, src=None):
        first = buf.at[1, body_rows, spans[c]] if src is None else src.at[0, :, spans[c]]
        final = buf.at[planes, body_rows, spans[c]] if src is None else src.at[planes - 1, :, spans[c]]
        return to_front(first, buf, n, c), to_back(final, buf, n, c)

    def row_copies(buf, a, b, n, src=None, c=0, span=whole_span):
        first = buf.at[a:b, low : low + 1, span] if src is None else src.at[:, 0:1, span]
        final = buf.at[a:b, high - 1 : high, span] if src is None else src.at[:, lines - 1 : lines, span]
        return (
            to_above(first, buf.at[a:b, high : high + 1, span], n, c),
            to_below(final, buf.at[a:b, low - 1 : low, span], n, c),
        )

    def start_faces(copies):
        pl.when(d > 0)(lambda: copies[0].start())
        pl.when(d < slabs - 1)(lambda: copies[1].start())

    def start_rows(copies):
        pl.when(y > 0)(lambda: copies[0].start())
        pl.when(y < bands - 1)(lambda: copies[1].start())

    def arrive_faces(copies):
        pl.when(d < slabs - 1)(lambda: copies[0].wait_recv())
        pl.when(d > 0)(lambda: copies[1].wait_recv())

    def arrive_rows(copies):
        pl.when(y < bands - 1)(lambda: copies[0].wait_recv())
        pl.when(y > 0)(lambda: copies[1].wait_recv())

    def sent_faces(copies):
        pl.when(d > 0)(lambda: copies[0].wait_send())
        pl.when(d < slabs - 1)(lambda: copies[1].wait_send())

    def sent_rows(copies):
        pl.when(y > 0)(lambda: copies[0].wait_send())
        pl.when(y < bands - 1)(lambda: copies[1].wait_send())

    faces = [
        [face_copies(buf, n, c, src) for c in range(CHUNKS)]
        for n, (buf, src) in enumerate([(fb, f_in), (kb, k_in), (ub, None), (sb, None)])
    ]

    def end_rows(buf, n):
        return [
            [row_copies(buf, a, a + 1, n + i, None, c, spans[c]) for i, a in enumerate((1, planes))] for c in range(CHUNKS)
        ]

    rows = [
        row_copies(fb, 1, last, 0, f_in),
        row_copies(kb, 1, last, 1, k_in),
        row_copies(ub, 2, planes, 2),
        row_copies(sb, 2, planes, 5),
    ]
    u_ends, s_ends = end_rows(ub, 3), end_rows(sb, 6)
    for c in range(CHUNKS):
        start_faces(faces[0][c])
        start_faces(faces[1][c])
    start_rows(rows[0])
    start_rows(rows[1])

    lane = lax.broadcasted_iota(jnp.int32, (BLOCK, columns), 1)
    row = lax.broadcasted_iota(jnp.int32, (BLOCK, columns), 0)
    at_start, at_end = lane == 0, lane == columns - 1
    at_top, at_bottom = row == 0, row == BLOCK - 1
    blocks = [low + BLOCK * i for i in range(lines // BLOCK)]
    edge_blocks, mid_blocks = (blocks[0], blocks[-1]), tuple(blocks[1:-1])

    def lower(ref, p, r):
        if r == blocks[-1]:
            v = ref[p, r : r + BLOCK, :]
            return jnp.where(at_bottom, v, pltpu.roll(v, BLOCK - 1, 0))
        return ref[p, r + 1 : r + 1 + BLOCK, :]

    loads[0].wait()

    def prepare(p, carry):
        for r in blocks:
            local = slice(r - low, r - low + BLOCK)
            k = kb[p + 1, r : r + BLOCK, :]
            ax[p, local, :] = k + jnp.where(at_end, 0.0, pltpu.roll(k, columns - 1, 1))
            ay[p, r : r + BLOCK, :] = k + lower(kb, p + 1, r)
            sg[p, local, :] = 0.5 + 0.5 * jnp.tanh(2.0 * k - 1.0)
        return carry

    lax.fori_loop(0, planes, prepare, 0)
    loads[1].wait()
    loads[2].wait()

    def react(src, dst, p, front=True, back=True):
        for r in blocks:
            here = slice(r, r + BLOCK)
            local = slice(r - low, r - low + BLOCK)
            u = src[p + 1, here, :]
            k = kb[p + 1, here, :]
            right = jnp.where(at_end, 0.0, pltpu.roll(u, columns - 1, 1))
            out = ax[p, local, :] * (right - u)
            flux = out - jnp.where(at_start, k * u, pltpu.roll(out, 1, 1))
            if front:
                flux = flux + (k + kb[p, here, :]) * (src[p, here, :] - u)
            if back:
                flux = flux + (k + kb[p + 2, here, :]) * (src[p + 2, here, :] - u)
            flux = flux + ay[p, here, :] * (lower(src, p + 1, r) - u)
            if r == low:
                above = jnp.where(at_top, u, pltpu.roll(u, 1, 0))
                flux = flux + (k + jnp.where(at_top, k, pltpu.roll(k, 1, 0))) * (above - u)
            else:
                flux = flux + ay[p, r - 1 : r - 1 + BLOCK, :] * (src[p + 1, r - 1 : r - 1 + BLOCK, :] - u)
            rate = STEP * rb[p, local, :]
            dst[p + 1, here, :] = u + (0.5 * STEP) * flux + rate * (jnp.tanh(u) - 0.5 * u)

    def react_all(src, dst):
        over(*inner, lambda p: react(src, dst, p))
        react(src, dst, 0, front=False)
        react(src, dst, planes - 1, back=False)

    def add_rows(src, dst, p, span=whole_span):
        for edge, outside in ((low, low - 1), (high - 1, high)):
            edge, outside = (slice(edge, edge + 1), span), (slice(outside, outside + 1), span)
            face = kb[p + 1, *edge] + kb[p + 1, *outside]
            dst[p + 1, *edge] += (0.5 * STEP) * face * (src[p + 1, *outside] - src[p + 1, *edge])

    def add_faces(src, dst, c):
        for edge, outside in ((1, 0), (planes, last)):
            for r in blocks:
                here = slice(r, r + BLOCK), spans[c]
                face = kb[edge, *here] + kb[outside, *here]
                dst[edge, *here] += (0.5 * STEP) * face * (src[outside, *here] - src[edge, *here])

    def over(start, count, stride, body):
        def lap(i, carry):
            body(start + stride * i)
            return carry

        lax.fori_loop(0, count, lap, 0)

    inner = (1, planes - 2, 1)
    outer = (0, 2, planes - 1)

    react_all(fb, ub)
    arrive_rows(rows[0])
    arrive_rows(rows[1])
    over(*inner, lambda p: add_rows(fb, ub, p))
    start_rows(rows[2])
    tell(0)
    over(*outer, lambda p: add_rows(fb, ub, p))
    for c in range(CHUNKS):
        arrive_faces(faces[0][c])
        arrive_faces(faces[1][c])
        add_faces(fb, ub, c)
        start_faces(faces[2][c])
        for copies in u_ends[c]:
            start_rows(copies)

    hear(0)
    tell(1)
    react_all(ub, sb)
    hear(1)
    tell(2)
    arrive_rows(rows[2])
    over(*inner, lambda p: add_rows(ub, sb, p))
    start_rows(rows[3])
    for c in range(CHUNKS):
        for copies in u_ends[c]:
            arrive_rows(copies)
        over(*outer, lambda p: add_rows(ub, sb, p, spans[c]))
        arrive_faces(faces[2][c])
        add_faces(ub, sb, c)
        start_faces(faces[3][c])
        for copies in s_ends[c]:
            start_rows(copies)
    hear(2)
    tell(3)
    store = pltpu.make_async_copy(sb.at[1:last, body_rows, :], stepped, load_sem.at[3])
    store.start()

    def lit(g_depth, g_row, g_col):
        norm = g_depth * g_depth + g_row * g_row + g_col * g_col
        facing = jnp.abs(0.36 * g_depth + 0.45 * g_row + 0.48 * g_col)
        return 0.25 + facing * lax.rsqrt(jnp.maximum(norm, 4.0))

    def across(p, r):
        u = sb[p + 1, r : r + BLOCK, :]
        right = jnp.where(at_end, 0.0, pltpu.roll(u, columns - 1, 1))
        return right - jnp.where(at_start, 0.0, pltpu.roll(u, 1, 1))

    def matter(p, r):
        rise = jnp.exp(2.0 * sb[p + 1, r : r + BLOCK, :])
        whole = 1.0 + rise
        passed = jnp.exp(-density * jnp.log(whole))
        opacity = 1.0 - passed
        return opacity, opacity * (rise / whole), opacity * sg[p, r - low : r - low + BLOCK, :], passed

    def shade(p, r):
        here = slice(r, r + BLOCK)
        g_depth = sb[p + 2, here, :] - sb[p, here, :]
        g_row = sb[p + 1, r + 1 : r + 1 + BLOCK, :] - sb[p + 1, r - 1 : r - 1 + BLOCK, :]
        light = lit(g_depth, g_row, across(p, r))
        opacity, red, green, passed = matter(p, r)
        red = light * red
        return red, light * green, light * opacity - red, passed

    def shade_inner(p, some):
        for r in some:
            local = slice(r - low, r - low + BLOCK)
            through = acc[3, local, :]
            red, green, blue, passed = shade(p, r)
            acc[0, local, :] += through * red
            acc[1, local, :] += through * green
            acc[2, local, :] += through * blue
            acc[3, local, :] = through * passed

    acc[0:3] = jnp.zeros((3, lines, columns), jnp.float32)
    acc[3] = jnp.ones((lines, columns), jnp.float32)
    over(*inner, lambda p: shade_inner(p, mid_blocks))

    for r in blocks:
        local = slice(r - low, r - low + BLOCK)
        for q, p in enumerate((0, planes - 1)):
            gc[q, local, :] = across(p, r)
            opacity, red, green, passed = matter(p, r)
            ends[q, 0, local, :] = red
            ends[q, 1, local, :] = green
            ends[q, 2, local, :] = opacity - red
            ends[q, 3, local, :] = passed

    hear(3)
    tell(4)
    arrive_rows(rows[3])
    over(*inner, lambda p: shade_inner(p, edge_blocks))
    for r in blocks:
        local = slice(r - low, r - low + BLOCK)
        passed = ends[0, 3, local, :]
        through = passed * acc[3, local, :]
        for i in range(3):
            acc[i, local, :] = passed * acc[i, local, :]
            ends[1, i, local, :] = through * ends[1, i, local, :]
        acc[3, local, :] = through * ends[1, 3, local, :]

    partner = {"depth": chip * 2 + 1 - core}

    def pair_copy(t):
        part = pl.ds(t * per_tile, per_tile)
        return pltpu.make_async_remote_copy(
            pieces.at[part, 2], pieces.at[part, core], pair_send.at[t], pair_recv.at[t], device_id=partner
        )

    order = []
    for i in (lanes_x // 2, 1, lanes_x - 1, 0):
        for h in (1, 0):
            side = lax.rem(z // per_tile + h, 2)
            order.append(lax.rem(x + i, lanes_x) * 2 + side)

    def span(t):
        return pl.ds(pl.multiple_of(t * TILE, TILE), TILE)

    pass_copy = pltpu.make_async_remote_copy(
        front_pass.at[1], front_pass.at[1], pass_sem.at[0], pass_sem.at[1], device_id=partner
    )

    @pl.when(core == 0)
    def _():
        for t in range(tiles):
            stack = jnp.concatenate([acc[3, :, t * TILE : (t + 1) * TILE]] * 4, axis=0)
            turned = stack.T.reshape(per_tile, 2, width, 4 * lines)
            part = slice(t * per_tile, (t + 1) * per_tile)
            front_pass[0, part] = turned[:, 0]
            front_pass[1, part] = turned[:, 1]
        pass_copy.start()

    for c in range(CHUNKS):
        arrive_faces(faces[3][c])
        for copies in s_ends[c]:
            arrive_rows(copies)

    def light_of(p, q, cols):
        g_depth = sb[p + 2, body_rows, cols] - sb[p, body_rows, cols]
        g_row = sb[p + 1, low + 1 : high + 1, cols] - sb[p + 1, low - 1 : high - 1, cols]
        return lit(g_depth, g_row, gc[q, :, cols])

    for t in order:
        cols = span(t)
        first = light_of(0, 0, cols)
        final = light_of(planes - 1, 1, cols)
        stack = [acc[c, :, cols] + first * ends[0, c, :, cols] + final * ends[1, c, :, cols] for c in range(3)]
        stack = jnp.concatenate(stack + [acc[3, :, cols]], axis=0)
        turned = stack.T.reshape(per_tile, 2, width, 4 * lines)
        part = pl.ds(t * per_tile, per_tile)
        pieces[part, 2 * core] = turned[:, 0]
        pieces[part, 2 - core] = turned[:, 1]
        pair_copy(t).start()

    colour_lane = lax.broadcasted_iota(jnp.int32, (width, 4 * lines), 1) < 3 * lines

    def part_copy(to, slot):
        return pltpu.make_async_remote_copy(
            comb.at[to], seg.at[slot], part_send.at[0], part_recv.at[0], device_id={"depth": to * 2 + core}
        )

    def all_parts():
        others = pl.ds(0, chips - 1)
        return pltpu.make_async_remote_copy(
            comb.at[others], seg.at[others], part_send.at[0], part_recv.at[0], device_id={"depth": d}
        )

    hear(rounds - 1)
    pl.when(core == 1)(lambda: pass_copy.wait_recv())
    for t in order:
        pair_copy(t).wait_recv()
        for q in range(per_tile):
            m = t * per_tile + q
            front = pieces[m, 0]
            comb[m] = front_pass[core, m] * pieces[m, 1] + jnp.where(colour_lane, front, 0.0)
        for q in range(per_tile):
            m = t * per_tile + q
            pl.when(m != chip)(lambda: part_copy(m, chip).start())
    seg[chip] = comb[chip]

    all_parts().wait_recv()
    all_parts().wait_send()

    def finish_pairs(t, carry):
        pair_copy(t).wait_send()
        return carry

    lax.fori_loop(0, tiles, finish_pairs, 0)
    pl.when(core == 0)(lambda: pass_copy.wait_send())
    for copies in sum(faces, []):
        sent_faces(copies)
    for copies in rows + sum(u_ends + s_ends, []):
        sent_rows(copies)
    store.wait()


def finish(near, parts, stepped, image, picture, sems):
    chips, width, wide = parts.shape
    lines = wide // 4
    field_copy = pltpu.make_async_copy(near, stepped, sems.at[0])
    field_copy.start()
    lane = lax.broadcasted_iota(jnp.int32, (width, wide), 1)
    total, through = jnp.zeros((width, wide), jnp.float32), jnp.ones((width, wide), jnp.float32)
    for m in range(chips):
        piece = parts[m]
        total = total + through * piece
        half = jnp.where(lane >= 3 * lines, piece, pltpu.roll(piece, 3 * lines, 1))
        through = through * jnp.where(lane >= 2 * lines, half, pltpu.roll(half, 2 * lines, 1))
    result = jnp.where(lane < 3 * lines, total, 1.0 - through)
    for c in range(4):
        picture[c] = result[:, c * lines : (c + 1) * lines]
    image_copy = pltpu.make_async_copy(picture, image, sems.at[1])
    image_copy.start()
    image_copy.wait()
    field_copy.wait()


def on_device(slabs, bands, field, coefficient, rate):
    planes, lines, columns = field.shape
    chips = slabs // 2
    width = columns // slabs
    padded = pltpu.VMEM((planes + 2, lines + 2 * TOP, columns), jnp.float32)
    plain = pltpu.VMEM((planes, lines, columns), jnp.float32)
    parts = pltpu.VMEM((chips, width, 4 * lines), jnp.float32)
    dma = pltpu.SemaphoreType.DMA
    near, gathered = pl.pallas_call(
        functools.partial(kernel, slabs, bands),
        out_shape=(
            jax.ShapeDtypeStruct(field.shape, jnp.float32),
            jax.ShapeDtypeStruct((chips, width, 4 * lines), jnp.float32),
        ),
        in_specs=[pl.BlockSpec(memory_space=pltpu.HBM)] * 3,
        out_specs=(pl.BlockSpec(memory_space=pl.ANY), pl.BlockSpec(memory_space=pltpu.VMEM)),
        scratch_shapes=[
            padded,
            padded,
            plain,
            padded,
            padded,
            plain,
            pltpu.VMEM((planes, lines + 2 * TOP, columns), jnp.float32),
            plain,
            pltpu.VMEM((4, lines, columns), jnp.float32),
            pltpu.VMEM((2, lines, columns), jnp.float32),
            pltpu.VMEM((2, 4, lines, columns), jnp.float32),
            pltpu.VMEM((chips, 3, width, 4 * lines), jnp.float32),
            pltpu.VMEM((2, chips, width, 4 * lines), jnp.float32),
            parts,
            dma((4,)),
            dma((4, 2, CHUNKS)),
            dma((4, 2, CHUNKS)),
            dma((8, 2, CHUNKS)),
            dma((8, 2, CHUNKS)),
            dma((columns // TILE,)),
            dma((columns // TILE,)),
            dma((1,)),
            dma((1,)),
            dma((2,)),
            pltpu.SemaphoreType.REGULAR((chips // RING // 2 + RING // 2 - 1, 2)),
        ],
        compiler_params=pltpu.CompilerParams(collective_id=0, has_side_effects=True, vmem_limit_bytes=40 << 20),
    )(*(pltpu.with_memory_space_constraint(v, pltpu.HBM) for v in (field, coefficient, rate)))
    stepped, image = pl.pallas_call(
        finish,
        out_shape=(
            jax.ShapeDtypeStruct(field.shape, jnp.float32),
            jax.ShapeDtypeStruct((4, width, lines), jnp.float32),
        ),
        in_specs=[pl.BlockSpec(memory_space=pl.ANY), pl.BlockSpec(memory_space=pltpu.VMEM)],
        out_specs=(pl.BlockSpec(memory_space=pltpu.HBM), pl.BlockSpec(memory_space=pltpu.HBM)),
        scratch_shapes=[pltpu.VMEM((4, width, lines), jnp.float32), dma((2,))],
        compiler_params=pltpu.CompilerParams(vmem_limit_bytes=8 << 20),
    )(near, gathered)
    return stepped, jnp.swapaxes(image, 1, 2)


def solution(mesh):
    return jax.shard_map(
        functools.partial(on_device, mesh.shape["depth"], mesh.shape["rows"]),
        mesh=mesh,
        in_specs=(P("depth", "rows", None),) * 3,
        out_specs=(P("depth", "rows", None), P(None, "rows", "depth")),
        check_vma=False,
    )
```

```python
import functools

import jax
import jax.numpy as jnp
from jax import lax
from jax.experimental import pallas as pl
from jax.experimental.pallas import tpu as pltpu
from jax.sharding import PartitionSpec as P

STEP = 0.15
TOP = 8
TILE = 128
BLOCK = 8
CHUNKS = 2
RING = 8


def kernel(
    slabs,
    bands,
    f_in,
    k_in,
    r_in,
    stepped,
    seg,
    fb,
    kb,
    rb,
    ub,
    sb,
    ax,
    ay,
    sg,
    acc,
    gc,
    ends,
    pieces,
    front_pass,
    comb,
    load_sem,
    face_send,
    face_recv,
    row_send,
    row_recv,
    pair_send,
    pair_recv,
    part_send,
    part_recv,
    pass_sem,
    known,
):
    d = lax.axis_index("depth")
    y = lax.axis_index("rows")
    planes, lines, columns = f_in.shape
    chips = slabs // 2
    width = columns // slabs
    tiles = columns // TILE
    per_tile = chips // tiles
    core = lax.rem(d, 2)
    chip = d // 2
    last = planes + 1
    low, high = TOP, TOP + lines
    density = 3.0 / (planes * slabs)
    body_rows = slice(low, high)
    spans = [slice(i * columns // CHUNKS, (i + 1) * columns // CHUNKS) for i in range(CHUNKS)]
    whole_span = slice(0, columns)

    loads = [
        pltpu.make_async_copy(src, dst, load_sem.at[i])
        for i, (src, dst) in enumerate(
            [
                (k_in, kb.at[1:last, body_rows, :]),
                (f_in, fb.at[1:last, body_rows, :]),
                (r_in, rb),
            ]
        )
    ]
    for copy in loads:
        copy.start()

    barrier = pltpu.get_barrier_semaphore()
    x, z = chip // RING, lax.rem(chip, RING)
    lanes_x = chips // RING

    def along_z(step):
        return (x * RING + lax.rem(z + step, RING)) * 2 + core

    def along_x(step):
        return (lax.rem(x + step, lanes_x) * RING + z) * 2 + core

    z_next, z_prev = along_z(1), along_z(RING - 1)
    x_next, x_prev = along_x(1), along_x(lanes_x - 1)
    for other in (lax.rem(d + 1, slabs), lax.rem(d + slabs - 1, slabs), z_next, z_prev, x_next, x_prev):
        pl.semaphore_signal(barrier, inc=1, device_id={"depth": other})
    for other in (lax.rem(y + 1, bands), lax.rem(y + bands - 1, bands)):
        pl.semaphore_signal(barrier, inc=1, device_id={"rows": other})

    z_rounds = RING // 2 - 1
    rounds = z_rounds + lanes_x // 2

    def tell(n):
        after, before = (z_next, z_prev) if n < z_rounds else (x_next, x_prev)
        pl.semaphore_signal(known.at[n, 0], inc=1, device_id={"depth": after})
        pl.semaphore_signal(known.at[n, 1], inc=1, device_id={"depth": before})

    def hear(n):
        pl.semaphore_wait(known.at[n, 0], 1)
        pl.semaphore_wait(known.at[n, 1], 1)

    def clear_planes(plane):
        for buf in (fb, kb, ub, sb):
            buf[plane, body_rows, :] = jnp.zeros((lines, columns), jnp.float32)

    def clear_rows(row):
        for buf in (fb, kb, ub, sb):
            buf[1:last, row : row + 1, :] = jnp.zeros((planes, 1, columns), jnp.float32)

    pl.when(d == 0)(lambda: clear_planes(0))
    pl.when(d == slabs - 1)(lambda: clear_planes(last))
    pl.when(y == 0)(lambda: clear_rows(low - 1))
    pl.when(y == bands - 1)(lambda: clear_rows(high))
    pl.semaphore_wait(barrier, 8)

    def to_front(src, dst, n, c):
        return pltpu.make_async_remote_copy(
            src, dst.at[last, body_rows, spans[c]], face_send.at[n, 0, c], face_recv.at[n, 0, c], device_id={"depth": d - 1}
        )

    def to_back(src, dst, n, c):
        return pltpu.make_async_remote_copy(
            src, dst.at[0, body_rows, spans[c]], face_send.at[n, 1, c], face_recv.at[n, 1, c], device_id={"depth": d + 1}
        )

    def to_above(src, dst, n, c):
        return pltpu.make_async_remote_copy(
            src, dst, row_send.at[n, 0, c], row_recv.at[n, 0, c], device_id={"rows": y - 1}
        )

    def to_below(src, dst, n, c):
        return pltpu.make_async_remote_copy(
            src, dst, row_send.at[n, 1, c], row_recv.at[n, 1, c], device_id={"rows": y + 1}
        )

    def face_copies(buf, n, c, src=None):
        first = buf.at[1, body_rows, spans[c]] if src is None else src.at[0, :, spans[c]]
        final = buf.at[planes, body_rows, spans[c]] if src is None else src.at[planes - 1, :, spans[c]]
        return to_front(first, buf, n, c), to_back(final, buf, n, c)

    def row_copies(buf, a, b, n, src=None, c=0, span=whole_span):
        first = buf.at[a:b, low : low + 1, span] if src is None else src.at[:, 0:1, span]
        final = buf.at[a:b, high - 1 : high, span] if src is None else src.at[:, lines - 1 : lines, span]
        return (
            to_above(first, buf.at[a:b, high : high + 1, span], n, c),
            to_below(final, buf.at[a:b, low - 1 : low, span], n, c),
        )

    def start_faces(copies):
        pl.when(d > 0)(lambda: copies[0].start())
        pl.when(d < slabs - 1)(lambda: copies[1].start())

    def start_rows(copies):
        pl.when(y > 0)(lambda: copies[0].start())
        pl.when(y < bands - 1)(lambda: copies[1].start())

    def arrive_faces(copies):
        pl.when(d < slabs - 1)(lambda: copies[0].wait_recv())
        pl.when(d > 0)(lambda: copies[1].wait_recv())

    def arrive_rows(copies):
        pl.when(y < bands - 1)(lambda: copies[0].wait_recv())
        pl.when(y > 0)(lambda: copies[1].wait_recv())

    def sent_faces(copies):
        pl.when(d > 0)(lambda: copies[0].wait_send())
        pl.when(d < slabs - 1)(lambda: copies[1].wait_send())

    def sent_rows(copies):
        pl.when(y > 0)(lambda: copies[0].wait_send())
        pl.when(y < bands - 1)(lambda: copies[1].wait_send())

    faces = [
        [face_copies(buf, n, c, src) for c in range(CHUNKS)]
        for n, (buf, src) in enumerate([(fb, f_in), (kb, k_in), (ub, None), (sb, None)])
    ]

    def end_rows(buf, n):
        return [
            [row_copies(buf, a, a + 1, n + i, None, c, spans[c]) for i, a in enumerate((1, planes))] for c in range(CHUNKS)
        ]

    rows = [
        row_copies(fb, 1, last, 0, f_in),
        row_copies(kb, 1, last, 1, k_in),
        row_copies(ub, 2, planes, 2),
        row_copies(sb, 2, planes, 5),
    ]
    u_ends, s_ends = end_rows(ub, 3), end_rows(sb, 6)
    for c in range(CHUNKS):
        start_faces(faces[0][c])
        start_faces(faces[1][c])
    start_rows(rows[0])
    start_rows(rows[1])
    tell(0)

    lane = lax.broadcasted_iota(jnp.int32, (BLOCK, columns), 1)
    row = lax.broadcasted_iota(jnp.int32, (BLOCK, columns), 0)
    at_start, at_end = lane == 0, lane == columns - 1
    at_top, at_bottom = row == 0, row == BLOCK - 1
    blocks = [low + BLOCK * i for i in range(lines // BLOCK)]
    edge_blocks, mid_blocks = (blocks[0], blocks[-1]), tuple(blocks[1:-1])

    def lower(ref, p, r):
        if r == blocks[-1]:
            v = ref[p, r : r + BLOCK, :]
            return jnp.where(at_bottom, v, pltpu.roll(v, BLOCK - 1, 0))
        return ref[p, r + 1 : r + 1 + BLOCK, :]

    loads[0].wait()

    def prepare(p, carry):
        for r in blocks:
            local = slice(r - low, r - low + BLOCK)
            k = kb[p + 1, r : r + BLOCK, :]
            ax[p, local, :] = k + jnp.where(at_end, 0.0, pltpu.roll(k, columns - 1, 1))
            ay[p, r : r + BLOCK, :] = k + lower(kb, p + 1, r)
            sg[p, local, :] = 0.5 + 0.5 * jnp.tanh(2.0 * k - 1.0)
        return carry

    lax.fori_loop(0, planes, prepare, 0)
    hear(0)
    tell(1)
    loads[1].wait()
    loads[2].wait()

    def react(src, dst, p, front=True, back=True):
        for r in blocks:
            here = slice(r, r + BLOCK)
            local = slice(r - low, r - low + BLOCK)
            u = src[p + 1, here, :]
            k = kb[p + 1, here, :]
            right = jnp.where(at_end, 0.0, pltpu.roll(u, columns - 1, 1))
            out = ax[p, local, :] * (right - u)
            flux = out - jnp.where(at_start, k * u, pltpu.roll(out, 1, 1))
            if front:
                flux = flux + (k + kb[p, here, :]) * (src[p, here, :] - u)
            if back:
                flux = flux + (k + kb[p + 2, here, :]) * (src[p + 2, here, :] - u)
            flux = flux + ay[p, here, :] * (lower(src, p + 1, r) - u)
            if r == low:
                above = jnp.where(at_top, u, pltpu.roll(u, 1, 0))
                flux = flux + (k + jnp.where(at_top, k, pltpu.roll(k, 1, 0))) * (above - u)
            else:
                flux = flux + ay[p, r - 1 : r - 1 + BLOCK, :] * (src[p + 1, r - 1 : r - 1 + BLOCK, :] - u)
            rate = STEP * rb[p, local, :]
            dst[p + 1, here, :] = u + (0.5 * STEP) * flux + rate * (jnp.tanh(u) - 0.5 * u)

    def react_all(src, dst):
        over(*inner, lambda p: react(src, dst, p))
        react(src, dst, 0, front=False)
        react(src, dst, planes - 1, back=False)

    def add_rows(src, dst, p, span=whole_span):
        for edge, outside in ((low, low - 1), (high - 1, high)):
            edge, outside = (slice(edge, edge + 1), span), (slice(outside, outside + 1), span)
            face = kb[p + 1, *edge] + kb[p + 1, *outside]
            dst[p + 1, *edge] += (0.5 * STEP) * face * (src[p + 1, *outside] - src[p + 1, *edge])

    def add_faces(src, dst, c):
        for edge, outside in ((1, 0), (planes, last)):
            for r in blocks:
                here = slice(r, r + BLOCK), spans[c]
                face = kb[edge, *here] + kb[outside, *here]
                dst[edge, *here] += (0.5 * STEP) * face * (src[outside, *here] - src[edge, *here])

    def over(start, count, stride, body):
        def lap(i, carry):
            body(start + stride * i)
            return carry

        lax.fori_loop(0, count, lap, 0)

    inner = (1, planes - 2, 1)
    outer = (0, 2, planes - 1)

    react_all(fb, ub)
    hear(1)
    tell(2)
    arrive_rows(rows[0])
    arrive_rows(rows[1])
    over(*inner, lambda p: add_rows(fb, ub, p))
    start_rows(rows[2])
    over(*outer, lambda p: add_rows(fb, ub, p))
    for c in range(CHUNKS):
        arrive_faces(faces[0][c])
        arrive_faces(faces[1][c])
        add_faces(fb, ub, c)
        start_faces(faces[2][c])
        for copies in u_ends[c]:
            start_rows(copies)
    hear(2)
    tell(3)

    react_all(ub, sb)
    hear(3)
    tell(4)
    arrive_rows(rows[2])
    over(*inner, lambda p: add_rows(ub, sb, p))
    start_rows(rows[3])
    for c in range(CHUNKS):
        for copies in u_ends[c]:
            arrive_rows(copies)
        over(*outer, lambda p: add_rows(ub, sb, p, spans[c]))
        arrive_faces(faces[2][c])
        add_faces(ub, sb, c)
        start_faces(faces[3][c])
        for copies in s_ends[c]:
            start_rows(copies)
    store = pltpu.make_async_copy(sb.at[1:last, body_rows, :], stepped, load_sem.at[3])
    store.start()

    def lit(g_depth, g_row, g_col):
        norm = g_depth * g_depth + g_row * g_row + g_col * g_col
        facing = jnp.abs(0.36 * g_depth + 0.45 * g_row + 0.48 * g_col)
        return 0.25 + facing * lax.rsqrt(jnp.maximum(norm, 4.0))

    def across(p, r):
        u = sb[p + 1, r : r + BLOCK, :]
        right = jnp.where(at_end, 0.0, pltpu.roll(u, columns - 1, 1))
        return right - jnp.where(at_start, 0.0, pltpu.roll(u, 1, 1))

    def matter(p, r):
        rise = jnp.exp(2.0 * sb[p + 1, r : r + BLOCK, :])
        whole = 1.0 + rise
        passed = jnp.exp(-density * jnp.log(whole))
        opacity = 1.0 - passed
        return opacity, opacity * (rise / whole), opacity * sg[p, r - low : r - low + BLOCK, :], passed

    def shade(p, r):
        here = slice(r, r + BLOCK)
        g_depth = sb[p + 2, here, :] - sb[p, here, :]
        g_row = sb[p + 1, r + 1 : r + 1 + BLOCK, :] - sb[p + 1, r - 1 : r - 1 + BLOCK, :]
        light = lit(g_depth, g_row, across(p, r))
        opacity, red, green, passed = matter(p, r)
        red = light * red
        return red, light * green, light * opacity - red, passed

    def shade_inner(p, some):
        for r in some:
            local = slice(r - low, r - low + BLOCK)
            through = acc[3, local, :]
            red, green, blue, passed = shade(p, r)
            acc[0, local, :] += through * red
            acc[1, local, :] += through * green
            acc[2, local, :] += through * blue
            acc[3, local, :] = through * passed

    acc[0:3] = jnp.zeros((3, lines, columns), jnp.float32)
    acc[3] = jnp.ones((lines, columns), jnp.float32)
    over(*inner, lambda p: shade_inner(p, mid_blocks))

    for r in blocks:
        local = slice(r - low, r - low + BLOCK)
        for q, p in enumerate((0, planes - 1)):
            gc[q, local, :] = across(p, r)
            opacity, red, green, passed = matter(p, r)
            ends[q, 0, local, :] = red
            ends[q, 1, local, :] = green
            ends[q, 2, local, :] = opacity - red
            ends[q, 3, local, :] = passed

    arrive_rows(rows[3])
    over(*inner, lambda p: shade_inner(p, edge_blocks))
    for r in blocks:
        local = slice(r - low, r - low + BLOCK)
        passed = ends[0, 3, local, :]
        through = passed * acc[3, local, :]
        for i in range(3):
            acc[i, local, :] = passed * acc[i, local, :]
            ends[1, i, local, :] = through * ends[1, i, local, :]
        acc[3, local, :] = through * ends[1, 3, local, :]

    partner = {"depth": chip * 2 + 1 - core}

    def pair_copy(t):
        part = pl.ds(t * per_tile, per_tile)
        return pltpu.make_async_remote_copy(
            pieces.at[part, 2], pieces.at[part, core], pair_send.at[t], pair_recv.at[t], device_id=partner
        )

    order = []
    for i in (lanes_x // 2, 1, lanes_x - 1, 0):
        for h in (1, 0):
            side = lax.rem(z // per_tile + h, 2)
            order.append(lax.rem(x + i, lanes_x) * 2 + side)

    def span(t):
        return pl.ds(pl.multiple_of(t * TILE, TILE), TILE)

    pass_copy = pltpu.make_async_remote_copy(
        front_pass.at[1], front_pass.at[1], pass_sem.at[0], pass_sem.at[1], device_id=partner
    )

    @pl.when(core == 0)
    def _():
        for t in range(tiles):
            stack = jnp.concatenate([acc[3, :, t * TILE : (t + 1) * TILE]] * 4, axis=0)
            turned = stack.T.reshape(per_tile, 2, width, 4 * lines)
            part = slice(t * per_tile, (t + 1) * per_tile)
            front_pass[0, part] = turned[:, 0]
            front_pass[1, part] = turned[:, 1]
        pass_copy.start()

    for c in range(CHUNKS):
        arrive_faces(faces[3][c])
        for copies in s_ends[c]:
            arrive_rows(copies)

    def light_of(p, q, cols):
        g_depth = sb[p + 2, body_rows, cols] - sb[p, body_rows, cols]
        g_row = sb[p + 1, low + 1 : high + 1, cols] - sb[p + 1, low - 1 : high - 1, cols]
        return lit(g_depth, g_row, gc[q, :, cols])

    for t in order:
        cols = span(t)
        first = light_of(0, 0, cols)
        final = light_of(planes - 1, 1, cols)
        stack = [acc[c, :, cols] + first * ends[0, c, :, cols] + final * ends[1, c, :, cols] for c in range(3)]
        stack = jnp.concatenate(stack + [acc[3, :, cols]], axis=0)
        turned = stack.T.reshape(per_tile, 2, width, 4 * lines)
        part = pl.ds(t * per_tile, per_tile)
        pieces[part, 2 * core] = turned[:, 0]
        pieces[part, 2 - core] = turned[:, 1]
        pair_copy(t).start()

    colour_lane = lax.broadcasted_iota(jnp.int32, (width, 4 * lines), 1) < 3 * lines

    def part_copy(to, slot):
        return pltpu.make_async_remote_copy(
            comb.at[to], seg.at[slot], part_send.at[0], part_recv.at[0], device_id={"depth": to * 2 + core}
        )

    def all_parts():
        others = pl.ds(0, chips - 1)
        return pltpu.make_async_remote_copy(
            comb.at[others], seg.at[others], part_send.at[0], part_recv.at[0], device_id={"depth": d}
        )

    hear(rounds - 1)
    pl.when(core == 1)(lambda: pass_copy.wait_recv())
    for t in order:
        pair_copy(t).wait_recv()
        for q in range(per_tile):
            m = t * per_tile + q
            front = pieces[m, 0]
            comb[m] = front_pass[core, m] * pieces[m, 1] + jnp.where(colour_lane, front, 0.0)
        for q in range(per_tile):
            m = t * per_tile + q
            pl.when(m != chip)(lambda: part_copy(m, chip).start())
    seg[chip] = comb[chip]

    all_parts().wait_recv()
    all_parts().wait_send()

    def finish_pairs(t, carry):
        pair_copy(t).wait_send()
        return carry

    lax.fori_loop(0, tiles, finish_pairs, 0)
    pl.when(core == 0)(lambda: pass_copy.wait_send())
    for copies in sum(faces, []):
        sent_faces(copies)
    for copies in rows + sum(u_ends + s_ends, []):
        sent_rows(copies)
    store.wait()


def finish(near, parts, stepped, image, picture, sems):
    chips, width, wide = parts.shape
    lines = wide // 4
    field_copy = pltpu.make_async_copy(near, stepped, sems.at[0])
    field_copy.start()
    lane = lax.broadcasted_iota(jnp.int32, (width, wide), 1)
    total, through = jnp.zeros((width, wide), jnp.float32), jnp.ones((width, wide), jnp.float32)
    for m in range(chips):
        piece = parts[m]
        total = total + through * piece
        half = jnp.where(lane >= 3 * lines, piece, pltpu.roll(piece, 3 * lines, 1))
        through = through * jnp.where(lane >= 2 * lines, half, pltpu.roll(half, 2 * lines, 1))
    result = jnp.where(lane < 3 * lines, total, 1.0 - through)
    for c in range(4):
        picture[c] = result[:, c * lines : (c + 1) * lines]
    image_copy = pltpu.make_async_copy(picture, image, sems.at[1])
    image_copy.start()
    image_copy.wait()
    field_copy.wait()


def on_device(slabs, bands, field, coefficient, rate):
    planes, lines, columns = field.shape
    chips = slabs // 2
    width = columns // slabs
    padded = pltpu.VMEM((planes + 2, lines + 2 * TOP, columns), jnp.float32)
    plain = pltpu.VMEM((planes, lines, columns), jnp.float32)
    parts = pltpu.VMEM((chips, width, 4 * lines), jnp.float32)
    dma = pltpu.SemaphoreType.DMA
    near, gathered = pl.pallas_call(
        functools.partial(kernel, slabs, bands),
        out_shape=(
            jax.ShapeDtypeStruct(field.shape, jnp.float32),
            jax.ShapeDtypeStruct((chips, width, 4 * lines), jnp.float32),
        ),
        in_specs=[pl.BlockSpec(memory_space=pltpu.HBM)] * 3,
        out_specs=(pl.BlockSpec(memory_space=pl.ANY), pl.BlockSpec(memory_space=pltpu.VMEM)),
        scratch_shapes=[
            padded,
            padded,
            plain,
            padded,
            padded,
            plain,
            pltpu.VMEM((planes, lines + 2 * TOP, columns), jnp.float32),
            plain,
            pltpu.VMEM((4, lines, columns), jnp.float32),
            pltpu.VMEM((2, lines, columns), jnp.float32),
            pltpu.VMEM((2, 4, lines, columns), jnp.float32),
            pltpu.VMEM((chips, 3, width, 4 * lines), jnp.float32),
            pltpu.VMEM((2, chips, width, 4 * lines), jnp.float32),
            parts,
            dma((4,)),
            dma((4, 2, CHUNKS)),
            dma((4, 2, CHUNKS)),
            dma((8, 2, CHUNKS)),
            dma((8, 2, CHUNKS)),
            dma((columns // TILE,)),
            dma((columns // TILE,)),
            dma((1,)),
            dma((1,)),
            dma((2,)),
            pltpu.SemaphoreType.REGULAR((chips // RING // 2 + RING // 2 - 1, 2)),
        ],
        compiler_params=pltpu.CompilerParams(collective_id=0, has_side_effects=True, vmem_limit_bytes=40 << 20),
    )(*(pltpu.with_memory_space_constraint(v, pltpu.HBM) for v in (field, coefficient, rate)))
    stepped, image = pl.pallas_call(
        finish,
        out_shape=(
            jax.ShapeDtypeStruct(field.shape, jnp.float32),
            jax.ShapeDtypeStruct((4, width, lines), jnp.float32),
        ),
        in_specs=[pl.BlockSpec(memory_space=pl.ANY), pl.BlockSpec(memory_space=pltpu.VMEM)],
        out_specs=(pl.BlockSpec(memory_space=pltpu.HBM), pl.BlockSpec(memory_space=pltpu.HBM)),
        scratch_shapes=[pltpu.VMEM((4, width, lines), jnp.float32), dma((2,))],
        compiler_params=pltpu.CompilerParams(vmem_limit_bytes=8 << 20),
    )(near, gathered)
    return stepped, jnp.swapaxes(image, 1, 2)


def solution(mesh):
    return jax.shard_map(
        functools.partial(on_device, mesh.shape["depth"], mesh.shape["rows"]),
        mesh=mesh,
        in_specs=(P("depth", "rows", None),) * 3,
        out_specs=(P("depth", "rows", None), P(None, "rows", "depth")),
        check_vma=False,
    )
```
